512 devices in a mesh: seq: 128 (over x, z, core), head: 4 (over y).
Axes of the slice: x: 4, y: 4, z: 16, core: 2. Of those that a mesh axis runs over, the one named last changes fastest.
Arguments:
- query_in: bfloat16 [65536, 256], P('seq', 'head'), may hold values from -6 to 6
- key_in: bfloat16 [65536, 256], P('seq', 'head'), may hold values from -6 to 6
- value_in: bfloat16 [65536, 2048], P('seq', 'head'), may hold values from -8 to 8
- conv_query: float32 [3, 256], P(None, 'head'), may hold values from -3.5 to 3.5
- conv_key: float32 [3, 256], P(None, 'head'), may hold values from -3.5 to 3.5
- conv_value: float32 [3, 2048], P(None, 'head'), may hold values from -3.5 to 3.5
- out_proj: bfloat16 [2048, 2048], P('head'), may hold values from -0.125 to 0.125
- out_grad: bfloat16 [65536, 2048], P(('seq', 'head')), may hold values from -8 to 8
Outputs:
- mixed: bfloat16 [65536, 2048], P(('seq', 'head'))
- grad_query: float32 [65536, 256], P('seq', 'head')
- grad_key: float32 [65536, 256], P('seq', 'head')
- grad_value: float32 [65536, 2048], P('seq', 'head')
- grad_conv_query: float32 [3, 256], P(None, 'head')
- grad_conv_key: float32 [3, 256], P(None, 'head')
- grad_conv_value: float32 [3, 2048], P(None, 'head')
The draws below stay inside these ranges and needn't reach their ends.
All inputs are finite; a program needn't handle non-finite values.
Results may differ from the reference program's by a relative error of at most 0.0049.
Values may be sent and summed in bfloat16 or wider, within the bound.
No kernel may reach another device: no remote copies, remote signals or barrier semaphores. Data moves between devices by JAX's collectives and lax.ppermute only.
A program may use at most 192 MiB of HBM per device.

```python
import math
import jax
import jax.numpy as jnp
import numpy as np
from jax import lax

D = 2048
HEADS = 16
FK = 16
VD = 128
FEAT = 153
TOKENS = 65536


def offset_field(key, row_count, col_count):
    subkeys = jax.random.split(key, 3)
    channel_mean = jax.random.normal(subkeys[0], (1, col_count), jnp.float32)
    offsets = jax.random.normal(subkeys[1], (row_count // 64, 1, col_count), jnp.float32)
    jitter = jax.random.normal(subkeys[2], (row_count // 64, 64, col_count), jnp.float32)
    values_all = (jitter + offsets).reshape(row_count, col_count) + channel_mean
    return jnp.clip(values_all, -8.0, 8.0)


def draw_value_in(key, part):
    return offset_field(jax.random.fold_in(key, 3), TOKENS, HEADS * VD).astype(jnp.bfloat16)


def draw_out_grad(key, part):
    return offset_field(jax.random.fold_in(key, 5), TOKENS, D).astype(jnp.bfloat16)


def block_levels(stream_key, dims, pieces, low, top_value):
    loudness, own = 1.0, jax.random.fold_in(stream_key, 6)
    for position, blocks in pieces:
        steps = jnp.exp(jax.random.uniform(jax.random.fold_in(own, position), (blocks,), jnp.float32, low / len(pieces), top_value / len(pieces)))
        loudness = loudness * jnp.repeat(steps, dims[position] // blocks).reshape([-1 if axis == position else 1 for axis in range(len(dims))])
    return loudness


def gaussian(rng, shape, scale, bound, shards=(), held_as=jnp.bfloat16):
    loudness = block_levels(rng, shape, shards, -0.22, 0.18) if shards else 1.0
    result = jax.random.normal(rng, shape, jnp.float32) * scale * loudness
    return jnp.minimum(jnp.maximum(result, -bound), bound).astype(held_as)


def setup_inputs(seed: int = 0) -> dict:
    seeds = jax.random.split(jax.random.key(seed), 9)
    return {
        "query_in": gaussian(seeds[0], (TOKENS, HEADS * FK), 1.0, 6.0, ((0, 128), (1, 4))),
        "key_in": gaussian(seeds[1], (TOKENS, HEADS * FK), 1.0, 6.0, ((0, 128), (1, 4))),
        "value_in": draw_value_in(jax.random.fold_in(seeds[8], 71), 0),
        "conv_query": gaussian(seeds[3], (3, HEADS * FK), 3 ** -0.5, 3.5, ((1, 4),), jnp.float32),
        "conv_key": gaussian(seeds[4], (3, HEADS * FK), 3 ** -0.5, 3.5, ((1, 4),), jnp.float32),
        "conv_value": gaussian(seeds[5], (3, HEADS * VD), 3 ** -0.5, 3.5, ((1, 4),), jnp.float32),
        "out_proj": gaussian(seeds[6], (HEADS * VD, D), (HEADS * VD) ** -0.5, 0.125, ((0, 4),)),
        "out_grad": draw_out_grad(jax.random.fold_in(seeds[8], 71), 0),
    }


HIGHEST = lax.Precision.HIGHEST

def pair_table(feature_dim):
    mapping = np.zeros((feature_dim * feature_dim, feature_dim * (feature_dim + 1) // 2), np.float32)
    column = 0
    for row_index in range(feature_dim):
        for col_index in range(row_index, feature_dim):
            if row_index == col_index:
                mapping[row_index * feature_dim + col_index, column] = 1.0 / math.sqrt(2.0 * feature_dim)
            else:
                mapping[row_index * feature_dim + col_index, column] = 1.0 / math.sqrt(feature_dim)
            column = column + 1
    return mapping

def features(inputs):
    feature_dim = inputs.shape[-1]
    linear = inputs * feature_dim ** (-0.25)
    products = (inputs[..., :, None] * inputs[..., None, :]).reshape(inputs.shape[:-1] + (feature_dim * feature_dim,))
    quadratic = jnp.dot(products, jnp.asarray(pair_table(feature_dim)).astype(inputs.dtype), precision=HIGHEST)
    constant = jnp.ones(inputs.shape[:-1] + (1,), inputs.dtype)
    return jnp.concatenate([constant, linear, quadratic], axis=-1)

def causal_conv(extended, weights, length):
    total = weights[0] * extended[2:length + 2]
    total = total + weights[1] * extended[1:length + 1]
    return total + weights[2] * extended[0:length]

def padded(inputs):
    return jnp.concatenate([jnp.zeros((2, inputs.shape[1]), jnp.float32), inputs], axis=0)

def attention_step(carry, block_inputs):
    state, norm_sum = carry
    query_blk, key_blk, value_blk = block_inputs
    phi_query = features(query_blk)
    phi_key = features(key_blk)
    block_len = query_blk.shape[0]
    causal = (lax.broadcasted_iota(jnp.int32, (block_len, block_len), 0) >= lax.broadcasted_iota(jnp.int32, (block_len, block_len), 1)).astype(jnp.float32)
    similarity = jnp.einsum('thf,shf->hts', query_blk, key_blk, precision=HIGHEST) * FK ** (-0.5)
    weights = (1.0 + similarity + 0.5 * similarity * similarity) * causal
    numerator = jnp.einsum('hts,shv->thv', weights, value_blk, precision=HIGHEST) + jnp.einsum('thf,hfv->thv', phi_query, state, precision=HIGHEST)
    denominator = lax.optimization_barrier(jnp.sum(weights, axis=2)).T + jnp.einsum('thf,hf->th', phi_query, norm_sum, precision=HIGHEST)
    state = state + jnp.einsum('shf,shv->hfv', phi_key, value_blk, precision=HIGHEST)
    norm_sum = norm_sum + lax.optimization_barrier(jnp.sum(phi_key, axis=0))
    return ((state, norm_sum), numerator / denominator[:, :, None])

def mixer(query_f, key_f, value_f, conv_query, conv_key, conv_value):
    length = query_f.shape[0]
    query_conv = causal_conv(padded(query_f), conv_query, length)
    key_conv = causal_conv(padded(key_f), conv_key, length)
    value_conv = causal_conv(padded(value_f), conv_value, length)
    block_rows = math.gcd(length, 512)
    block_count = length // block_rows
    query_blocks = query_conv.reshape(block_count, block_rows, HEADS, FK)
    key_blocks = key_conv.reshape(block_count, block_rows, HEADS, FK)
    value_blocks = value_conv.reshape(block_count, block_rows, HEADS, VD)
    start_state = (jnp.zeros((HEADS, FEAT, VD), jnp.float32), jnp.zeros((HEADS, FEAT), jnp.float32))
    final_carry, outputs = lax.scan(jax.checkpoint(attention_step), start_state, (query_blocks, key_blocks, value_blocks))
    return outputs.reshape(length, HEADS, VD)

def reference(query_in, key_in, value_in, conv_query, conv_key, conv_value, out_proj, out_grad):
    attended, pullback = jax.vjp(mixer, query_in.astype(jnp.float32), key_in.astype(jnp.float32), value_in.astype(jnp.float32), conv_query, conv_key, conv_value)
    length = attended.shape[0]
    flat_attended = attended.reshape(length, HEADS * VD).astype(jnp.bfloat16)
    mixed = jnp.dot(flat_attended, out_proj, preferred_element_type=jnp.float32).astype(jnp.bfloat16)
    upstream = jnp.dot(out_grad, out_proj.T, preferred_element_type=jnp.float32).reshape(length, HEADS, VD)
    grads = pullback(upstream)
    return (mixed, grads[0], grads[1], grads[2], grads[3], grads[4], grads[5])
```

```python
import jax
import jax.numpy as jnp
import numpy as np
from jax import lax
from jax.experimental import pallas as pl
from jax.experimental.pallas import tpu as pltpu
from jax.sharding import Mesh, PartitionSpec as P

FK = 16
VD = 128
FEAT = 153
ROWS = 160
WIDE = 256
SUMS = FEAT

SEQ = ("x", "z", "core")
HIGHEST = lax.Precision.HIGHEST
F32 = jnp.float32
BF16 = jnp.bfloat16


def tables():
    places = np.full((8, WIDE), -1, np.int32)
    factors = np.zeros((8, WIDE), np.float32)
    factors[0, 0] = 1.0
    factors[0, 1 : FK + 1] = 0.25
    places[0, 1 : FK + 1] = np.arange(FK)
    factors[1, 0] = 1.0
    factors[2, : FK + 1] = 1.0
    column = FK + 1
    for i in range(FK):
        for j in range(i, FK):
            places[0, column], places[1, column] = i, j
            factors[0, column] = 1.0 / 32.0 if i == j else 1.0 / 16.0
            column += 1
    return places, factors


def mm(a, b, ca, cb):
    return lax.dot_general(a, b, (((ca,), (cb,)), ((), ())), preferred_element_type=F32)


def halves(x):
    high = x.astype(BF16)
    return high, (x - high.astype(F32)).astype(BF16)


def fold(pair):
    return pair[:, :VD] + pair[:, VD:]


def selectors(places, head):
    row = lax.broadcasted_iota(jnp.int32, (WIDE, WIDE), 0)
    own = (((row >> 4) & 3) == head) & (row < 192)
    channel = row & 15
    first = jnp.where(own & (channel == places[0:1, :]), 1.0, 0.0).astype(BF16)
    second = jnp.where(own & (channel == places[1:2, :]), 1.0, 0.0).astype(BF16)
    return first, second


def head_lanes(head, width):
    lane = lax.broadcasted_iota(jnp.int32, (1, width), 1)
    return jnp.where(((lane >> 4) & 3) == head, 1.0, 0.0)


def expand(pieces, select, factors):
    return (
        mm(pieces, select[0], 1, 0) + factors[1:2, :],
        mm(pieces, select[1], 1, 0) + factors[2:3, :],
    )


def pull(grad_first, grad_second, select):
    return mm(grad_first.astype(BF16), select[0][:64, :], 1, 1) + mm(
        grad_second.astype(BF16), select[1][:64, :], 1, 1
    )


def pack(state, total):
    row = lax.broadcasted_iota(jnp.int32, (ROWS, VD), 0)
    state = jnp.where(row == SUMS, total[:, :VD], state[:ROWS, :])
    return jnp.where(row == SUMS + 1, total[:, VD:], state)


def unpack(packed):
    total = jnp.concatenate([packed[SUMS : SUMS + 1, :], packed[SUMS + 1 : SUMS + 2, :]], axis=1)
    return jnp.concatenate([packed, jnp.zeros((WIDE - ROWS, VD), F32)], axis=0), total


def similar(query_pieces, key_pieces, head):
    mine = (query_pieces.astype(F32) * head_lanes(head, WIDE)).astype(BF16)
    return mm(mine, key_pieces, 1, 1) * 0.25


def direct(high, low):
    return high[:, :64] + high[:, 64:128] + low[:, :64]


def causal_mask(length):
    return lax.broadcasted_iota(jnp.int32, (length, length), 0) >= lax.broadcasted_iota(
        jnp.int32, (length, length), 1
    )


def extend(scratch, rows, rim):
    length = rows.shape[0]
    scratch[0:8, :] = jnp.concatenate([jnp.zeros((6, rows.shape[1]), F32), rim], axis=0)
    scratch[8 : length + 8, :] = rows.astype(F32)


def convolve(scratch, taps, length):
    total = taps[0:1, :] * scratch[8 : length + 8, :]
    total = total + taps[1:2, :] * scratch[7 : length + 7, :]
    return total + taps[2:3, :] * scratch[6 : length + 6, :]


def first_kernel(
    q_in, k_in, v_in, rim_qk, rim_v, taps_q, taps_k, taps_v, places, factors,
    q4, k4, k5, vb, state, narrow, broad,
):
    head = pl.program_id(0)
    length = q_in.shape[0]

    @pl.when(head == 0)
    def _():
        rim = rim_qk[...].astype(F32)
        for source, taps, edge, target in (
            (q_in, taps_q, rim[:, :64], q4),
            (k_in, taps_k, rim[:, 64:], k4),
        ):
            extend(narrow, source[...], edge)
            x = convolve(narrow, taps[...], length)
            high = x.astype(BF16).astype(F32)
            rest = x - high
            mid = rest.astype(BF16).astype(F32)
            low = rest - mid
            target[:, :128] = jnp.concatenate([high, mid], axis=1).astype(BF16)
            target[:, 128:] = jnp.concatenate([low, high], axis=1).astype(BF16)
            if target is k4:
                k5[:, :128] = jnp.concatenate([high, high], axis=1).astype(BF16)
                k5[:, 128:] = jnp.concatenate([high, mid], axis=1).astype(BF16)

    extend(broad, v_in[...], rim_v[...].astype(F32))
    value = jnp.concatenate(halves(convolve(broad, taps_v[...], length)), axis=1)
    vb[...] = value
    first, second = expand(k4[...], selectors(places[...], head), factors[...])
    phi = (first * second).astype(BF16)
    state[...] = pack(
        fold(mm(phi, value, 0, 0)), jnp.sum(phi.astype(F32), axis=0, keepdims=True)
    )


def local_kernel(q4, k5, vb, numer, denom):
    head = pl.program_id(0)
    a = similar(q4[...], k5[...], head)
    length = a.shape[0]
    weight = jnp.where(causal_mask(length), 1.0 + a + 0.5 * a * a, 0.0)
    high, low = halves(weight)
    value = vb[...]
    numer[...] = fold(mm(high, value, 1, 0)) + mm(low, value[:, :VD], 1, 0)
    denom[...] = jnp.broadcast_to(jnp.sum(weight, axis=1, keepdims=True), (length, VD))


def middle_kernel(q4, before, numer, denom, up, places, factors, att, ng, dg, state):
    head = pl.program_id(0)
    scale = factors[...]
    first, second = expand(q4[...], selectors(places[...], head), scale)
    phi = first * second * scale[0:1, :]
    high, low = halves(phi)
    seen, total = unpack(before[...])
    seen_high, seen_low = halves(seen)
    inter = mm(high, seen_high, 1, 0) + mm(high, seen_low, 1, 0) + mm(low, seen_high, 1, 0)
    inverse = 1.0 / (denom[...] + jnp.sum(phi * total, axis=1, keepdims=True))
    out = (numer[...] + inter) * inverse
    att[...] = out.astype(BF16)
    upstream = up[...]
    numer_grad = upstream * inverse
    denom_grad = -jnp.sum(numer_grad * out, axis=1, keepdims=True)
    ng[...] = numer_grad
    dg[...] = jnp.broadcast_to(denom_grad, dg.shape)
    state[...] = pack(
        mm(high, numer_grad.astype(BF16), 0, 0),
        jnp.sum(high.astype(F32) * denom_grad, axis=0, keepdims=True),
    )


def inner_kernel(q4, k4, k5, vb, before, ng, dg, places, factors, gq, kd, gv):
    head = pl.program_id(0)
    scale = factors[...]
    query, value = q4[...], vb[...]
    a = similar(query, k5[...], head)
    mask = causal_mask(a.shape[0])
    numer_grad = ng[...]
    denom_grad = dg[:, 0:1]
    high, low = halves(numer_grad)
    both = jnp.concatenate([high, low], axis=1)
    value_high, value_low = value[:, :VD], value[:, VD:]
    weight_grad = (
        mm(both, jnp.concatenate([value_high, value_high], axis=1), 1, 1)
        + mm(high, value_low, 1, 1)
        + denom_grad
    )
    sim_high, sim_low = halves(jnp.where(mask, weight_grad * (0.25 + 0.25 * a), 0.0))
    weight = jnp.where(mask, 1.0 + a + 0.5 * a * a, 0.0).astype(BF16)
    gv[...] = mm(weight, high, 0, 0)
    lanes = head_lanes(head, 64)
    key = k4[...]
    query_direct = direct(mm(sim_high, key, 1, 0), mm(sim_low, key, 1, 0)) * lanes
    key_direct = direct(mm(sim_high, query, 0, 0), mm(sim_low, query, 0, 0)) * lanes
    select = selectors(places[...], head)
    first, second = expand(query, select, scale)
    seen, total = unpack(before[...])
    seen_high, seen_low = halves(seen)
    phi_grad = (
        mm(both, jnp.concatenate([seen_high, seen_high], axis=1), 1, 1)
        + mm(high, seen_low, 1, 1)
        + denom_grad * total
    ) * scale[0:1, :]
    query_grad = query_direct + pull(phi_grad * second, phi_grad * first, select)

    @pl.when(head == 0)
    def _():
        gq[...] = query_grad
        kd[...] = key_direct

    @pl.when(head > 0)
    def _():
        gq[...] += query_grad
        kd[...] += key_direct


def conv_back(scratch, grad, taps, length):
    scratch[0:length, :] = grad
    scratch[length : length + 8, :] = jnp.zeros((8, grad.shape[1]), F32)
    return (
        taps[0:1, :] * grad
        + taps[1:2, :] * scratch[1 : length + 1, :]
        + taps[2:3, :] * scratch[2 : length + 2, :]
    )


def edges(scratch, grad, length):
    sums = [
        jnp.sum(grad * scratch[8 - tap : length + 8 - tap, :], axis=0, keepdims=True)
        for tap in range(3)
    ]
    return jnp.concatenate(sums + [sums[0], grad[0:4, :]], axis=0)


def last_kernel(
    q_in, k_in, v_in, rim_qk, rim_v, taps_q, taps_k, taps_v, places, factors,
    k4, vb, after, gq, kd, gv_in, grad_q, grad_k, grad_v, edge_qk, edge_v, narrow, broad, gk,
):
    head = pl.program_id(0)
    length = q_in.shape[0]
    later, total = unpack(after[...])
    later_high, later_low = halves(later)
    value = vb[...]
    value_high = value[:, :VD]
    select = selectors(places[...], head)
    first, second = expand(k4[...], select, factors[...])
    phi_grad = (
        mm(
            jnp.concatenate([value_high, value_high], axis=1),
            jnp.concatenate([later_high, later_low], axis=1),
            1,
            1,
        )
        + mm(value[:, VD:], later_high, 1, 1)
        + total
    )
    key_grad = pull(phi_grad * second, phi_grad * first, select)

    @pl.when(head == 0)
    def _():
        gk[...] = kd[...] + key_grad

    @pl.when(head > 0)
    def _():
        gk[...] += key_grad

    value_grad = gv_in[...] + mm((first * second).astype(BF16), later_high, 1, 0)
    grad_v[...] = conv_back(broad, value_grad, taps_v[...], length)
    extend(broad, v_in[...], rim_v[...].astype(F32))
    edge_v[...] = edges(broad, value_grad, length)

    @pl.when(head == pl.num_programs(0) - 1)
    def _():
        rim = rim_qk[...].astype(F32)
        found = []
        for source, taps, edge, grad, target in (
            (q_in, taps_q, rim[:, :64], gq[...], grad_q),
            (k_in, taps_k, rim[:, 64:], gk[...], grad_k),
        ):
            target[...] = conv_back(narrow, grad, taps[...], length)
            extend(narrow, source[...], edge)
            found.append(edges(narrow, grad, length))
        edge_qk[...] = jnp.concatenate(found, axis=1)


def rim_kernel(tail, taps_q, taps_k, taps_v, q_in, k_in, v_in, grad_q, grad_k, grad_v):
    tails = tail[...]
    for start, taps, source, target in (
        (0, taps_q, q_in, grad_q),
        (64, taps_k, k_in, grad_k),
        (128, taps_v, v_in, grad_v),
    ):
        width = taps.shape[1]
        row = lax.broadcasted_iota(jnp.int32, (8, width), 0)
        one, two = tails[0:1, start : start + width], tails[1:2, start : start + width]
        weights = taps[...]
        extra = jnp.where(row == 6, weights[2:3, :] * one, 0.0)
        extra = extra + jnp.where(row == 7, weights[1:2, :] * one + weights[2:3, :] * two, 0.0)
        target[...] = source[...] + extra


def from_behind(block, axis, distance):
    devices = range(lax.axis_size(axis))
    route = [(i - distance, i) for i in devices if i - distance in devices]
    return lax.ppermute(block, axis, route)


def carried_in(packed, reverse):
    ranks = lax.axis_size(SEQ)
    everyone = lax.all_to_all(packed.reshape(ranks, -1), SEQ, 0, 0, tiled=True)
    rows = lax.broadcasted_iota(jnp.int32, (ranks, ranks), 0)
    cols = lax.broadcasted_iota(jnp.int32, (ranks, ranks), 1)
    reached = (cols > rows) if reverse else (cols < rows)
    sums = jnp.dot(reached.astype(F32), everyone, precision=HIGHEST)
    return lax.all_to_all(sums, SEQ, 0, 0, tiled=True).reshape(packed.shape)


def turned(block, axis, distance):
    size = lax.axis_size(axis)
    return lax.ppermute(block, axis, [(i, (i + distance) % size) for i in range(size)])


def gathered(block, axis):
    size, index, rows = lax.axis_size(axis), lax.axis_index(axis), block.shape[0]
    whole = jnp.zeros((size * rows,) + block.shape[1:], block.dtype)
    for distance in range(size):
        part = turned(block, axis, distance) if distance else block
        source = (index - distance) % size
        whole = lax.dynamic_update_slice_in_dim(whole, part, source * rows, 0)
    return whole


def scattered(whole, axis):
    size, index = lax.axis_size(axis), lax.axis_index(axis)
    rows = whole.shape[0] // size
    total = lax.dynamic_slice_in_dim(whole, index * rows, rows, 0)
    for distance in range(1, size):
        target = (index + distance) % size
        part = lax.dynamic_slice_in_dim(whole, target * rows, rows, 0)
        total = total + turned(part, axis, distance)
    return total


def to_all(block, axis):
    copies = jnp.broadcast_to(block[None], (lax.axis_size(axis),) + block.shape)
    return lax.all_to_all(copies, axis, 0, 0, tiled=True)


def body(query_in, key_in, value_in, conv_query, conv_key, conv_value, out_proj, out_grad):
    length, keys = query_in.shape
    heads = conv_value.shape[1] // VD
    assert keys == heads * FK == 64
    places, factors = (jnp.asarray(t) for t in tables())

    def whole(*shape):
        return pl.BlockSpec(shape, lambda h: (0,) * len(shape))

    def per_head(rows):
        return pl.BlockSpec((rows, VD), lambda h: (0, h))

    pairs = pl.BlockSpec((length, 2 * VD), lambda h: (0, h))
    packs = pl.BlockSpec((ROWS, VD), lambda h: (h, 0))
    table = whole(8, WIDE)
    pieces = whole(length, WIDE)
    narrow = whole(length, keys)

    def arr(rows, cols, dtype=F32):
        return jax.ShapeDtypeStruct((rows, cols), dtype)

    def call(kernel, name, ins, outs, shapes, flops, scratch=()):
        return pl.pallas_call(
            kernel,
            name=name,
            grid=(heads,),
            in_specs=ins,
            out_specs=outs,
            out_shape=shapes,
            scratch_shapes=list(scratch),
            cost_estimate=pl.CostEstimate(
                flops=flops, bytes_accessed=4 << 20, transcendentals=0
            ),
        )

    values = heads * VD
    rim = from_behind(
        jnp.concatenate([x[length - 2 :] for x in (query_in, key_in, value_in)], axis=1), SEQ, 1
    )
    rim_qk, rim_v = rim[:, : 2 * keys], rim[:, 2 * keys :]
    conv_ins = [
        narrow, narrow, per_head(length), whole(2, 2 * keys), per_head(2),
        whole(3, keys), whole(3, keys), per_head(3), table, table,
    ]
    conv_args = (
        query_in, key_in, value_in, rim_qk, rim_v,
        conv_query, conv_key, conv_value, places, factors,
    )
    buffers = [pltpu.VMEM((length + 8, keys), F32), pltpu.VMEM((length + 8, VD), F32)]
    q4, k4, k5, vb, local_state = call(
        first_kernel, "first", conv_ins,
        [pieces, pieces, pieces, pairs, packs],
        [arr(length, WIDE, BF16)] * 3 + [arr(length, 2 * values, BF16), arr(heads * ROWS, VD)],
        2 << 30, buffers,
    )(*conv_args)
    cotangent = gathered(out_grad, "head")
    upstream = lax.dot_general(
        cotangent, out_proj, (((1,), (1,)), ((), ())), preferred_element_type=F32
    )
    numer, denom = call(
        local_kernel, "local", [pieces, pieces, pairs],
        [per_head(length)] * 2, [arr(length, values)] * 2, 4 << 30,
    )(q4, k5, vb)
    before = carried_in(local_state, False)
    att, ng, dg, grad_state = call(
        middle_kernel, "middle",
        [pieces, packs] + [per_head(length)] * 3 + [table, table],
        [per_head(length)] * 3 + [packs],
        [arr(length, values, BF16), arr(length, values), arr(length, values)]
        + [arr(heads * ROWS, VD)],
        4 << 30,
    )(q4, before, numer, denom, upstream, places, factors)
    after = carried_in(grad_state, True)
    gq, kd, gv = call(
        inner_kernel, "inner",
        [pieces] * 3 + [pairs, packs] + [per_head(length)] * 2 + [table, table],
        [narrow, narrow, per_head(length)],
        [arr(length, keys)] * 2 + [arr(length, values)],
        8 << 30,
    )(q4, k4, k5, vb, before, ng, dg, places, factors)
    partial = jnp.dot(att, out_proj, preferred_element_type=F32)
    mixed = scattered(partial, "head").astype(BF16)
    grad_query, grad_key, grad_value, edge_qk, edge_v = call(
        last_kernel, "last",
        conv_ins + [pieces, pairs, packs, narrow, narrow, per_head(length)],
        [narrow, narrow, per_head(length), whole(8, 2 * keys), per_head(8)],
        [arr(length, keys)] * 2 + [arr(length, values), arr(8, 2 * keys), arr(8, values)],
        4 << 30, buffers + [pltpu.VMEM((length, keys), F32)],
    )(*conv_args, k4, vb, after, gq, kd, gv)
    edge = jnp.concatenate([edge_qk, edge_v], axis=1)
    tail = from_behind(edge[4:6], SEQ, -1)
    taps = lax.psum(edge[:3], "core")
    taps = jnp.sum(to_all(taps, "z").reshape(lax.axis_size("z"), 3, -1), axis=0)
    taps = lax.psum(taps, "x")
    last = length // 8 - 1
    rims = [pl.BlockSpec((8, n), lambda i: (last, 0)) for n in (keys, keys, values)]
    grad_query, grad_key, grad_value = pl.pallas_call(
        rim_kernel,
        name="rims",
        grid=(1,),
        in_specs=[whole(2, 2 * keys + values), whole(3, keys), whole(3, keys), whole(3, values)]
        + rims,
        out_specs=rims,
        out_shape=[arr(length, keys)] * 2 + [arr(length, values)],
        input_output_aliases={4: 0, 5: 1, 6: 2},
    )(tail, conv_query, conv_key, conv_value, grad_query, grad_key, grad_value)
    return (
        mixed,
        grad_query,
        grad_key,
        grad_value,
        taps[:, :keys],
        taps[:, keys : 2 * keys],
        taps[:, 2 * keys :],
    )


def refined(mesh):
    ranks, groups = mesh.devices.shape
    shape = (4, 16, 2, groups) if ranks == 128 else (1, ranks // 2, 2, groups)
    return Mesh(mesh.devices.reshape(shape), SEQ + ("head",))


def solution(mesh):
    mesh = refined(mesh)
    in_specs = (
        P(SEQ, "head"),
        P(SEQ, "head"),
        P(SEQ, "head"),
        P(None, "head"),
        P(None, "head"),
        P(None, "head"),
        P("head", None),
        P(SEQ + ("head",), None),
    )
    out_specs = (
        P(SEQ + ("head",), None),
        P(SEQ, "head"),
        P(SEQ, "head"),
        P(SEQ, "head"),
        P(None, "head"),
        P(None, "head"),
        P(None, "head"),
    )
    return jax.shard_map(body, mesh=mesh, in_specs=in_specs, out_specs=out_specs, check_vma=False)
```

```python
import jax
import jax.numpy as jnp
import numpy as np
from jax import lax
from jax.experimental import pallas as pl
from jax.experimental.pallas import tpu as pltpu
from jax.sharding import Mesh, PartitionSpec as P

FK = 16
VD = 128
FEAT = 153
ROWS = 160
WIDE = 256
SUMS = FEAT

SEQ = ("x", "z", "core")
HIGHEST = lax.Precision.HIGHEST
F32 = jnp.float32
BF16 = jnp.bfloat16


def tables():
    places = np.full((8, WIDE), -1, np.int32)
    factors = np.zeros((8, WIDE), np.float32)
    factors[0, 0] = 1.0
    factors[0, 1 : FK + 1] = 0.25
    places[0, 1 : FK + 1] = np.arange(FK)
    factors[1, 0] = 1.0
    factors[2, : FK + 1] = 1.0
    column = FK + 1
    for i in range(FK):
        for j in range(i, FK):
            places[0, column], places[1, column] = i, j
            factors[0, column] = 1.0 / 32.0 if i == j else 1.0 / 16.0
            column += 1
    return places, factors


def mm(a, b, ca, cb):
    return lax.dot_general(a, b, (((ca,), (cb,)), ((), ())), preferred_element_type=F32)


def halves(x):
    high = x.astype(BF16)
    return high, (x - high.astype(F32)).astype(BF16)


def fold(pair):
    return pair[:, :VD] + pair[:, VD:]


def selectors(places, head):
    row = lax.broadcasted_iota(jnp.int32, (WIDE, WIDE), 0)
    own = (((row >> 4) & 3) == head) & (row < 192)
    channel = row & 15
    first = jnp.where(own & (channel == places[0:1, :]), 1.0, 0.0).astype(BF16)
    second = jnp.where(own & (channel == places[1:2, :]), 1.0, 0.0).astype(BF16)
    return first, second


def head_lanes(head, width):
    lane = lax.broadcasted_iota(jnp.int32, (1, width), 1)
    return jnp.where(((lane >> 4) & 3) == head, 1.0, 0.0)


def expand(pieces, select, factors):
    return (
        mm(pieces, select[0], 1, 0) + factors[1:2, :],
        mm(pieces, select[1], 1, 0) + factors[2:3, :],
    )


def pull(grad_first, grad_second, select):
    return mm(grad_first.astype(BF16), select[0][:64, :], 1, 1) + mm(
        grad_second.astype(BF16), select[1][:64, :], 1, 1
    )


def pack(state, total):
    row = lax.broadcasted_iota(jnp.int32, (ROWS, VD), 0)
    state = jnp.where(row == SUMS, total[:, :VD], state[:ROWS, :])
    return jnp.where(row == SUMS + 1, total[:, VD:], state)


def unpack(packed):
    total = jnp.concatenate([packed[SUMS : SUMS + 1, :], packed[SUMS + 1 : SUMS + 2, :]], axis=1)
    return jnp.concatenate([packed, jnp.zeros((WIDE - ROWS, VD), F32)], axis=0), total


def similar(query_pieces, key_pieces, head):
    mine = (query_pieces.astype(F32) * head_lanes(head, WIDE)).astype(BF16)
    return mm(mine, key_pieces, 1, 1) * 0.25


def direct(high, low):
    return high[:, :64] + high[:, 64:128] + low[:, :64]


def causal_mask(length):
    return lax.broadcasted_iota(jnp.int32, (length, length), 0) >= lax.broadcasted_iota(
        jnp.int32, (length, length), 1
    )


def extend(scratch, rows, rim):
    length = rows.shape[0]
    scratch[0:8, :] = jnp.concatenate([jnp.zeros((6, rows.shape[1]), F32), rim], axis=0)
    scratch[8 : length + 8, :] = rows.astype(F32)


def convolve(scratch, taps, length):
    total = taps[0:1, :] * scratch[8 : length + 8, :]
    total = total + taps[1:2, :] * scratch[7 : length + 7, :]
    return total + taps[2:3, :] * scratch[6 : length + 6, :]


def first_kernel(
    q_in, k_in, v_in, rim_qk, rim_v, taps_q, taps_k, taps_v, places, factors,
    q4, k4, k5, vb, state, narrow, broad,
):
    head = pl.program_id(0)
    length = q_in.shape[1]

    @pl.when(head == 0)
    def _():
        rim = rim_qk[...].astype(F32)
        for source, taps, edge, target in (
            (q_in, taps_q, rim[:, :64], q4),
            (k_in, taps_k, rim[:, 64:], k4),
        ):
            extend(narrow, source[...].astype(F32).T, edge)
            x = convolve(narrow, taps[...], length)
            high = x.astype(BF16).astype(F32)
            rest = x - high
            mid = rest.astype(BF16).astype(F32)
            low = rest - mid
            target[:, :128] = jnp.concatenate([high, mid], axis=1).astype(BF16)
            target[:, 128:] = jnp.concatenate([low, high], axis=1).astype(BF16)
            if target is k4:
                k5[:, :128] = jnp.concatenate([high, high], axis=1).astype(BF16)
                k5[:, 128:] = jnp.concatenate([high, mid], axis=1).astype(BF16)

    extend(broad, v_in[...], rim_v[...].astype(F32))
    value = jnp.concatenate(halves(convolve(broad, taps_v[...], length)), axis=1)
    vb[...] = value
    first, second = expand(k4[...], selectors(places[...], head), factors[...])
    phi = (first * second).astype(BF16)
    state[...] = pack(
        fold(mm(phi, value, 0, 0)), jnp.sum(phi.astype(F32), axis=0, keepdims=True)
    )


def local_kernel(q4, k5, vb, numer, denom):
    head = pl.program_id(0)
    a = similar(q4[...], k5[...], head)
    length = a.shape[0]
    weight = jnp.where(causal_mask(length), 1.0 + a + 0.5 * a * a, 0.0)
    high, low = halves(weight)
    value = vb[...]
    numer[...] = fold(mm(high, value, 1, 0)) + mm(low, value[:, :VD], 1, 0)
    denom[...] = jnp.broadcast_to(jnp.sum(weight, axis=1, keepdims=True), (length, VD))


def middle_kernel(q4, before, numer, denom, up, places, factors, att, ng, dg, state):
    head = pl.program_id(0)
    scale = factors[...]
    first, second = expand(q4[...], selectors(places[...], head), scale)
    phi = first * second * scale[0:1, :]
    high, low = halves(phi)
    seen, total = unpack(before[...])
    seen_high, seen_low = halves(seen)
    inter = mm(high, seen_high, 1, 0) + mm(high, seen_low, 1, 0) + mm(low, seen_high, 1, 0)
    inverse = 1.0 / (denom[...] + jnp.sum(phi * total, axis=1, keepdims=True))
    out = (numer[...] + inter) * inverse
    att[...] = out.astype(BF16)
    upstream = up[...]
    numer_grad = upstream * inverse
    denom_grad = -jnp.sum(numer_grad * out, axis=1, keepdims=True)
    ng[...] = numer_grad
    dg[...] = jnp.broadcast_to(denom_grad, dg.shape)
    state[...] = pack(
        mm(high, numer_grad.astype(BF16), 0, 0),
        jnp.sum(high.astype(F32) * denom_grad, axis=0, keepdims=True),
    )


def inner_kernel(q4, k4, k5, vb, before, ng, dg, places, factors, gq, kd, gv):
    head = pl.program_id(0)
    scale = factors[...]
    query, value = q4[...], vb[...]
    a = similar(query, k5[...], head)
    mask = causal_mask(a.shape[0])
    numer_grad = ng[...]
    denom_grad = dg[:, 0:1]
    high, low = halves(numer_grad)
    both = jnp.concatenate([high, low], axis=1)
    value_high, value_low = value[:, :VD], value[:, VD:]
    weight_grad = (
        mm(both, jnp.concatenate([value_high, value_high], axis=1), 1, 1)
        + mm(high, value_low, 1, 1)
        + denom_grad
    )
    sim_high, sim_low = halves(jnp.where(mask, weight_grad * (0.25 + 0.25 * a), 0.0))
    weight = jnp.where(mask, 1.0 + a + 0.5 * a * a, 0.0).astype(BF16)
    gv[...] = mm(weight, high, 0, 0)
    lanes = head_lanes(head, 64)
    key = k4[...]
    query_direct = direct(mm(sim_high, key, 1, 0), mm(sim_low, key, 1, 0)) * lanes
    key_direct = direct(mm(sim_high, query, 0, 0), mm(sim_low, query, 0, 0)) * lanes
    select = selectors(places[...], head)
    first, second = expand(query, select, scale)
    seen, total = unpack(before[...])
    seen_high, seen_low = halves(seen)
    phi_grad = (
        mm(both, jnp.concatenate([seen_high, seen_high], axis=1), 1, 1)
        + mm(high, seen_low, 1, 1)
        + denom_grad * total
    ) * scale[0:1, :]
    query_grad = query_direct + pull(phi_grad * second, phi_grad * first, select)

    @pl.when(head == 0)
    def _():
        gq[...] = query_grad
        kd[...] = key_direct

    @pl.when(head > 0)
    def _():
        gq[...] += query_grad
        kd[...] += key_direct


def conv_back(scratch, grad, taps, length):
    scratch[0:length, :] = grad
    scratch[length : length + 8, :] = jnp.zeros((8, grad.shape[1]), F32)
    return (
        taps[0:1, :] * grad
        + taps[1:2, :] * scratch[1 : length + 1, :]
        + taps[2:3, :] * scratch[2 : length + 2, :]
    )


def tap_sums(scratch, grad, length):
    return jnp.concatenate(
        [
            jnp.sum(grad * scratch[8 - tap : length + 8 - tap, :], axis=0, keepdims=True)
            for tap in range(3)
        ],
        axis=0,
    )


def last_kernel(
    q_in, k_in, v_in, rim_qk, rim_v, taps_q, taps_k, taps_v, places, factors,
    k4, vb, after, gq, kd, gv_in, grad_q, grad_k, grad_v, taps_out, heads_first, narrow, broad, gk,
):
    head = pl.program_id(0)
    length = q_in.shape[1]
    later, total = unpack(after[...])
    later_high, later_low = halves(later)
    value = vb[...]
    value_high = value[:, :VD]
    select = selectors(places[...], head)
    first, second = expand(k4[...], select, factors[...])
    phi_grad = (
        mm(
            jnp.concatenate([value_high, value_high], axis=1),
            jnp.concatenate([later_high, later_low], axis=1),
            1,
            1,
        )
        + mm(value[:, VD:], later_high, 1, 1)
        + total
    )
    key_grad = pull(phi_grad * second, phi_grad * first, select)

    @pl.when(head == 0)
    def _():
        gk[...] = kd[...] + key_grad

    @pl.when(head > 0)
    def _():
        gk[...] += key_grad

    value_grad = gv_in[...] + mm((first * second).astype(BF16), later_high, 1, 0)
    grad_v[...] = conv_back(broad, value_grad, taps_v[...], length)
    extend(broad, v_in[...], rim_v[...].astype(F32))
    sums = tap_sums(broad, value_grad, length)
    heads = heads_first.shape[1] // VD - 1
    for index in range(heads):

        @pl.when(head == index)
        def _(index=index):
            taps_out[3 * index : 3 * index + 3, :] = sums
            heads_first[:, (index + 1) * VD : (index + 2) * VD] = value_grad[0:2, :]

    @pl.when(head == pl.num_programs(0) - 1)
    def _():
        rim = rim_qk[...].astype(F32)
        found = []
        for source, taps, edge, grad, target in (
            (q_in, taps_q, rim[:, :64], gq[...], grad_q),
            (k_in, taps_k, rim[:, 64:], gk[...], grad_k),
        ):
            target[...] = conv_back(narrow, grad, taps[...], length).T
            extend(narrow, source[...].astype(F32).T, edge)
            found.append(tap_sums(narrow, grad, length))
        taps_out[3 * heads : 3 * heads + 3, :] = jnp.concatenate(found, axis=1)
        taps_out[3 * heads + 3 :, :] = jnp.zeros((13 - 3 * heads, VD), F32)
        heads_first[:, :VD] = jnp.concatenate([gq[0:2, :], gk[0:2, :]], axis=1)


def rim_kernel(tail, taps_q, taps_k, taps_v, q_in, k_in, v_in, grad_q, grad_k, grad_v):
    tails = tail[...]
    for start, taps, source, target in (
        (0, taps_q, q_in, grad_q),
        (64, taps_k, k_in, grad_k),
        (128, taps_v, v_in, grad_v),
    ):
        width = taps.shape[1]
        row = lax.broadcasted_iota(jnp.int32, (8, width), 0)
        one, two = tails[0:1, start : start + width], tails[1:2, start : start + width]
        weights = taps[...]
        extra = jnp.where(row == 6, weights[2:3, :] * one, 0.0)
        extra = extra + jnp.where(row == 7, weights[1:2, :] * one + weights[2:3, :] * two, 0.0)
        if start < 128:
            extra = jnp.concatenate([jnp.zeros((120, width), F32), extra], axis=0).T
        target[...] = source[...] + extra


def from_behind(block, axis, distance):
    devices = range(lax.axis_size(axis))
    route = [(i - distance, i) for i in devices if i - distance in devices]
    return lax.ppermute(block, axis, route)


def carried_in(packed, reverse, ahead=()):
    ranks = lax.axis_size(SEQ)
    everyone = lax.all_to_all(packed.reshape(ranks, -1), SEQ, 0, 0, tiled=True)
    rows = lax.broadcasted_iota(jnp.int32, (ranks, ranks), 0)
    cols = lax.broadcasted_iota(jnp.int32, (ranks, ranks), 1)
    reached = (cols > rows) if reverse else (cols < rows)
    sums = jnp.dot(reached.astype(F32), everyone, precision=HIGHEST)
    if ahead:
        sums, ahead = lax.optimization_barrier((sums, ahead))
    return lax.all_to_all(sums, SEQ, 0, 0, tiled=True).reshape(packed.shape), ahead


def turned(block, axis, distance):
    size = lax.axis_size(axis)
    return lax.ppermute(block, axis, [(i, (i + distance) % size) for i in range(size)])


def gathered(block, axis):
    size, index, rows = lax.axis_size(axis), lax.axis_index(axis), block.shape[0]
    whole = jnp.zeros((size * rows,) + block.shape[1:], block.dtype)
    for distance in range(size):
        part = turned(block, axis, distance) if distance else block
        source = (index - distance) % size
        whole = lax.dynamic_update_slice_in_dim(whole, part, source * rows, 0)
    return whole


def scattered(whole, axis):
    size, index = lax.axis_size(axis), lax.axis_index(axis)
    rows = whole.shape[0] // size
    total = lax.dynamic_slice_in_dim(whole, index * rows, rows, 0)
    for distance in range(1, size):
        target = (index + distance) % size
        part = lax.dynamic_slice_in_dim(whole, target * rows, rows, 0)
        total = total + turned(part, axis, distance)
    return total


def to_all(block, axis):
    copies = jnp.broadcast_to(block[None], (lax.axis_size(axis),) + block.shape)
    return lax.all_to_all(copies, axis, 0, 0, tiled=True)


def body(query_in, key_in, value_in, conv_query, conv_key, conv_value, out_proj, out_grad):
    length, keys = query_in.shape
    heads = conv_value.shape[1] // VD
    assert keys == heads * FK == 64
    places, factors = (jnp.asarray(t) for t in tables())

    def whole(*shape):
        return pl.BlockSpec(shape, lambda h: (0,) * len(shape))

    def per_head(rows):
        return pl.BlockSpec((rows, VD), lambda h: (0, h))

    pairs = pl.BlockSpec((length, 2 * VD), lambda h: (0, h))
    packs = pl.BlockSpec((ROWS, VD), lambda h: (h, 0))
    table = whole(8, WIDE)
    pieces = whole(length, WIDE)
    narrow = whole(length, keys)

    def arr(rows, cols, dtype=F32):
        return jax.ShapeDtypeStruct((rows, cols), dtype)

    def call(kernel, name, ins, outs, shapes, flops, scratch=()):
        return pl.pallas_call(
            kernel,
            name=name,
            grid=(heads,),
            in_specs=ins,
            out_specs=outs,
            out_shape=shapes,
            scratch_shapes=list(scratch),
            cost_estimate=pl.CostEstimate(
                flops=flops, bytes_accessed=4 << 20, transcendentals=0
            ),
        )

    values = heads * VD
    rim = from_behind(
        jnp.concatenate([x[length - 2 :] for x in (query_in, key_in, value_in)], axis=1), SEQ, 1
    )
    query_cols, key_cols = query_in.T, key_in.T
    upright = whole(keys, length)
    conv_ins = [
        upright, upright, per_head(length), whole(2, 2 * keys),
        pl.BlockSpec((2, VD), lambda h: (0, h + 1)),
        whole(3, keys), whole(3, keys), per_head(3), table, table,
    ]
    conv_args = (
        query_cols, key_cols, value_in, rim, rim,
        conv_query, conv_key, conv_value, places, factors,
    )
    buffers = [pltpu.VMEM((length + 8, keys), F32), pltpu.VMEM((length + 8, VD), F32)]
    q4, k4, k5, vb, local_state = call(
        first_kernel, "first", conv_ins,
        [pieces, pieces, pieces, pairs, packs],
        [arr(length, WIDE, BF16)] * 3 + [arr(length, 2 * values, BF16), arr(heads * ROWS, VD)],
        2 << 30, buffers,
    )(*conv_args)
    cotangent = gathered(out_grad, "head")
    upstream = lax.dot_general(
        cotangent, out_proj, (((1,), (1,)), ((), ())), preferred_element_type=F32
    )
    numer, denom = call(
        local_kernel, "local", [pieces, pieces, pairs],
        [per_head(length)] * 2, [arr(length, values)] * 2, 4 << 30,
    )(q4, k5, vb)
    before, _ = carried_in(local_state, False)
    att, ng, dg, grad_state = call(
        middle_kernel, "middle",
        [pieces, packs] + [per_head(length)] * 3 + [table, table],
        [per_head(length)] * 3 + [packs],
        [arr(length, values, BF16), arr(length, values), arr(length, values)]
        + [arr(heads * ROWS, VD)],
        4 << 30,
    )(q4, before, numer, denom, upstream, places, factors)
    gq, kd, gv = call(
        inner_kernel, "inner",
        [pieces] * 3 + [pairs, packs] + [per_head(length)] * 2 + [table, table],
        [narrow, narrow, per_head(length)],
        [arr(length, keys)] * 2 + [arr(length, values)],
        8 << 30,
    )(q4, k4, k5, vb, before, ng, dg, places, factors)
    after, (gq, kd, gv) = carried_in(grad_state, True, (gq, kd, gv))
    partial = jnp.dot(att, out_proj, preferred_element_type=F32)
    mixed = scattered(partial, "head").astype(BF16)
    grad_query, grad_key, grad_value, taps, first_rows = call(
        last_kernel, "last",
        conv_ins + [pieces, pairs, packs, narrow, narrow, per_head(length)],
        [upright, upright, per_head(length), whole(16, VD), whole(2, 2 * keys + values)],
        [arr(keys, length)] * 2
        + [arr(length, values), arr(16, VD), arr(2, 2 * keys + values)],
        4 << 30, buffers + [pltpu.VMEM((length, keys), F32)],
    )(*conv_args, k4, vb, after, gq, kd, gv)
    tail = from_behind(first_rows, SEQ, -1)
    for axis in ("z", ("x", "core")):
        everyone = to_all(taps, axis).reshape((lax.axis_size(axis),) + taps.shape)
        taps = jnp.sum(everyone, axis=0)
    rims = [
        pl.BlockSpec((keys, VD), lambda i: (0, length // VD - 1)),
        pl.BlockSpec((keys, VD), lambda i: (0, length // VD - 1)),
        pl.BlockSpec((8, values), lambda i: (length // 8 - 1, 0)),
    ]
    grad_query, grad_key, grad_value = pl.pallas_call(
        rim_kernel,
        name="rims",
        grid=(1,),
        in_specs=[whole(2, 2 * keys + values), whole(3, keys), whole(3, keys), whole(3, values)]
        + rims,
        out_specs=rims,
        out_shape=[arr(keys, length)] * 2 + [arr(length, values)],
        input_output_aliases={4: 0, 5: 1, 6: 2},
    )(tail, conv_query, conv_key, conv_value, grad_query, grad_key, grad_value)
    value_taps = taps[: 3 * heads].reshape(heads, 3, VD).transpose(1, 0, 2).reshape(3, values)
    other_taps = taps[3 * heads : 3 * heads + 3]
    return (
        mixed,
        grad_query.T,
        grad_key.T,
        grad_value,
        other_taps[:, :keys],
        other_taps[:, keys:],
        value_taps,
    )


def refined(mesh):
    ranks, groups = mesh.devices.shape
    shape = (4, 16, 2, groups) if ranks == 128 else (1, ranks // 2, 2, groups)
    return Mesh(mesh.devices.reshape(shape), SEQ + ("head",))


def solution(mesh):
    mesh = refined(mesh)
    in_specs = (
        P(SEQ, "head"),
        P(SEQ, "head"),
        P(SEQ, "head"),
        P(None, "head"),
        P(None, "head"),
        P(None, "head"),
        P("head", None),
        P(SEQ + ("head",), None),
    )
    out_specs = (
        P(SEQ + ("head",), None),
        P(SEQ, "head"),
        P(SEQ, "head"),
        P(SEQ, "head"),
        P(None, "head"),
        P(None, "head"),
        P(None, "head"),
    )
    return jax.shard_map(body, mesh=mesh, in_specs=in_specs, out_specs=out_specs, check_vma=False)
```

```python
import jax
import jax.numpy as jnp
import numpy as np
from jax import lax
from jax.experimental import pallas as pl
from jax.experimental.pallas import tpu as pltpu
from jax.sharding import Mesh, PartitionSpec as P

FK = 16
VD = 128
FEAT = 153
ROWS = 160
WIDE = 256
SUMS = FEAT

SEQ = ("x", "z", "core")
HIGHEST = lax.Precision.HIGHEST
F32 = jnp.float32
BF16 = jnp.bfloat16


def tables():
    places = np.full((8, WIDE), -1, np.int32)
    factors = np.zeros((8, WIDE), np.float32)
    factors[0, 0] = 1.0
    factors[0, 1 : FK + 1] = 0.25
    places[0, 1 : FK + 1] = np.arange(FK)
    factors[1, 0] = 1.0
    factors[2, : FK + 1] = 1.0
    column = FK + 1
    for i in range(FK):
        for j in range(i, FK):
            places[0, column], places[1, column] = i, j
            factors[0, column] = 1.0 / 32.0 if i == j else 1.0 / 16.0
            column += 1
    return places, factors


def mm(a, b, ca, cb):
    return lax.dot_general(a, b, (((ca,), (cb,)), ((), ())), preferred_element_type=F32)


def halves(x):
    high = x.astype(BF16)
    return high, (x - high.astype(F32)).astype(BF16)


def fold(pair):
    return pair[:, :VD] + pair[:, VD:]


def selectors(places, head):
    row = lax.broadcasted_iota(jnp.int32, (WIDE, WIDE), 0)
    own = (((row >> 4) & 3) == head) & (row < 192)
    channel = row & 15
    first = jnp.where(own & (channel == places[0:1, :]), 1.0, 0.0).astype(BF16)
    second = jnp.where(own & (channel == places[1:2, :]), 1.0, 0.0).astype(BF16)
    return first, second


def head_lanes(head, width):
    lane = lax.broadcasted_iota(jnp.int32, (1, width), 1)
    return jnp.where(((lane >> 4) & 3) == head, 1.0, 0.0)


def expand(pieces, select, factors):
    return (
        mm(pieces, select[0], 1, 0) + factors[1:2, :],
        mm(pieces, select[1], 1, 0) + factors[2:3, :],
    )


def pull(grad_first, grad_second, select):
    return mm(grad_first.astype(BF16), select[0][:64, :], 1, 1) + mm(
        grad_second.astype(BF16), select[1][:64, :], 1, 1
    )


def pack(state, total):
    row = lax.broadcasted_iota(jnp.int32, (ROWS, VD), 0)
    state = jnp.where(row == SUMS, total[:, :VD], state[:ROWS, :])
    return jnp.where(row == SUMS + 1, total[:, VD:], state)


def unpack(packed):
    total = jnp.concatenate([packed[SUMS : SUMS + 1, :], packed[SUMS + 1 : SUMS + 2, :]], axis=1)
    return jnp.concatenate([packed, jnp.zeros((WIDE - ROWS, VD), F32)], axis=0), total


def similar(query_pieces, key_pieces, head):
    mine = (query_pieces.astype(F32) * head_lanes(head, WIDE)).astype(BF16)
    return mm(mine, key_pieces, 1, 1) * 0.25


def direct(high, low):
    return high[:, :64] + high[:, 64:128] + low[:, :64]


def causal_mask(length):
    return lax.broadcasted_iota(jnp.int32, (length, length), 0) >= lax.broadcasted_iota(
        jnp.int32, (length, length), 1
    )


def extend(scratch, rows, rim):
    length = rows.shape[0]
    scratch[0:8, :] = rim
    scratch[8 : length + 8, :] = rows.astype(F32)


def convolve(scratch, taps, length):
    total = taps[0:1, :] * scratch[8 : length + 8, :]
    total = total + taps[1:2, :] * scratch[7 : length + 7, :]
    return total + taps[2:3, :] * scratch[6 : length + 6, :]


def rim_rows(q_in, k_in, v_in, out):
    pair = jnp.concatenate([q_in[...].astype(F32), k_in[...].astype(F32)], axis=0).T
    out[:, :VD] = pair[-16:, :].astype(BF16)
    out[:, VD:] = v_in[...]


def split_query(x, target):
    high = x.astype(BF16).astype(F32)
    rest = x - high
    mid = rest.astype(BF16).astype(F32)
    target[:, :128] = jnp.concatenate([high, mid], axis=1).astype(BF16)
    target[:, 128:] = jnp.concatenate([rest - mid, high], axis=1).astype(BF16)
    return high, mid


def split_key(x, target, similar_target):
    high, mid = split_query(x, target)
    similar_target[:, :128] = jnp.concatenate([high, high], axis=1).astype(BF16)
    similar_target[:, 128:] = jnp.concatenate([high, mid], axis=1).astype(BF16)


def first_kernel(
    q_in, k_in, v_in, taps_q, taps_k, taps_v, places, factors,
    q4, k4, k5, vb, state, narrow, broad,
):
    head = pl.program_id(0)
    length = q_in.shape[1]
    none = jnp.zeros((8, 1), F32)

    @pl.when(head == 0)
    def _():
        extend(narrow, q_in[...].astype(F32).T, jnp.broadcast_to(none, (8, 64)))
        split_query(convolve(narrow, taps_q[...], length), q4)
        extend(narrow, k_in[...].astype(F32).T, jnp.broadcast_to(none, (8, 64)))
        split_key(convolve(narrow, taps_k[...], length), k4, k5)

    extend(broad, v_in[...], jnp.broadcast_to(none, (8, VD)))
    value = jnp.concatenate(halves(convolve(broad, taps_v[...], length)), axis=1)
    vb[...] = value
    first, second = expand(k4[...], selectors(places[...], head), factors[...])
    known = lax.broadcasted_iota(jnp.int32, (length, WIDE), 0) >= 2
    phi = jnp.where(known, first * second, 0.0).astype(BF16)
    state[...] = pack(
        fold(mm(phi, value, 0, 0)), jnp.sum(phi.astype(F32), axis=0, keepdims=True)
    )


def mend_kernel(
    q_in, k_in, v_in, rim_qk, rim_v, taps_q, taps_k, taps_v, places, factors,
    q4_in, k4_in, k5_in, vb_in, state_in, q4, k4, k5, vb, state, narrow, broad,
):
    head = pl.program_id(0)

    @pl.when(head == 0)
    def _():
        rim = rim_qk[8:, :].astype(F32)
        extend(narrow, q_in[...].astype(F32).T[:16, :], rim[:, :64])
        split_query(convolve(narrow, taps_q[...], 16), q4)
        extend(narrow, k_in[...].astype(F32).T[:16, :], rim[:, 64:])
        split_key(convolve(narrow, taps_k[...], 16), k4, k5)

    extend(broad, v_in[...], rim_v[8:, :].astype(F32))
    value = jnp.concatenate(halves(convolve(broad, taps_v[...], 16)), axis=1)
    vb[...] = value
    first, second = expand(k4[...], selectors(places[...], head), factors[...])
    missing = lax.broadcasted_iota(jnp.int32, (16, WIDE), 0) < 2
    phi = jnp.where(missing, first * second, 0.0).astype(BF16)
    state[...] = state_in[...] + pack(
        fold(mm(phi, value, 0, 0)), jnp.sum(phi.astype(F32), axis=0, keepdims=True)
    )


def local_kernel(q4, k5, vb, numer, denom):
    head = pl.program_id(0)
    a = similar(q4[...], k5[...], head)
    length = a.shape[0]
    weight = jnp.where(causal_mask(length), 1.0 + a + 0.5 * a * a, 0.0)
    high, low = halves(weight)
    value = vb[...]
    numer[...] = fold(mm(high, value, 1, 0)) + mm(low, value[:, :VD], 1, 0)
    denom[...] = jnp.broadcast_to(jnp.sum(weight, axis=1, keepdims=True), (length, VD))


def middle_kernel(q4, before, numer, denom, up, places, factors, att, ng, dg, state):
    head = pl.program_id(0)
    scale = factors[...]
    first, second = expand(q4[...], selectors(places[...], head), scale)
    phi = first * second * scale[0:1, :]
    high, low = halves(phi)
    seen, total = unpack(before[...])
    seen_high, seen_low = halves(seen)
    inter = mm(high, seen_high, 1, 0) + mm(high, seen_low, 1, 0) + mm(low, seen_high, 1, 0)
    inverse = 1.0 / (denom[...] + jnp.sum(phi * total, axis=1, keepdims=True))
    out = (numer[...] + inter) * inverse
    att[...] = out.astype(BF16)
    upstream = up[...]
    numer_grad = upstream * inverse
    denom_grad = -jnp.sum(numer_grad * out, axis=1, keepdims=True)
    ng[...] = numer_grad
    dg[...] = jnp.broadcast_to(denom_grad, dg.shape)
    state[...] = pack(
        mm(high, numer_grad.astype(BF16), 0, 0),
        jnp.sum(high.astype(F32) * denom_grad, axis=0, keepdims=True),
    )


def inner_kernel(q4, k4, k5, vb, before, ng, dg, places, factors, gq, kd, gv):
    head = pl.program_id(0)
    scale = factors[...]
    query, value = q4[...], vb[...]
    a = similar(query, k5[...], head)
    mask = causal_mask(a.shape[0])
    numer_grad = ng[...]
    denom_grad = dg[:, 0:1]
    high, low = halves(numer_grad)
    both = jnp.concatenate([high, low], axis=1)
    value_high, value_low = value[:, :VD], value[:, VD:]
    weight_grad = (
        mm(both, jnp.concatenate([value_high, value_high], axis=1), 1, 1)
        + mm(high, value_low, 1, 1)
        + denom_grad
    )
    sim_high, sim_low = halves(jnp.where(mask, weight_grad * (0.25 + 0.25 * a), 0.0))
    weight = jnp.where(mask, 1.0 + a + 0.5 * a * a, 0.0).astype(BF16)
    gv[...] = mm(weight, high, 0, 0)
    lanes = head_lanes(head, 64)
    key = k4[...]
    query_direct = direct(mm(sim_high, key, 1, 0), mm(sim_low, key, 1, 0)) * lanes
    key_direct = direct(mm(sim_high, query, 0, 0), mm(sim_low, query, 0, 0)) * lanes
    select = selectors(places[...], head)
    first, second = expand(query, select, scale)
    seen, total = unpack(before[...])
    seen_high, seen_low = halves(seen)
    phi_grad = (
        mm(both, jnp.concatenate([seen_high, seen_high], axis=1), 1, 1)
        + mm(high, seen_low, 1, 1)
        + denom_grad * total
    ) * scale[0:1, :]
    query_grad = query_direct + pull(phi_grad * second, phi_grad * first, select)

    @pl.when(head == 0)
    def _():
        gq[...] = query_grad
        kd[...] = key_direct

    @pl.when(head > 0)
    def _():
        gq[...] += query_grad
        kd[...] += key_direct


def conv_back(scratch, grad, taps, length):
    scratch[0:length, :] = grad
    scratch[length : length + 8, :] = jnp.zeros((8, grad.shape[1]), F32)
    return (
        taps[0:1, :] * grad
        + taps[1:2, :] * scratch[1 : length + 1, :]
        + taps[2:3, :] * scratch[2 : length + 2, :]
    )


def tap_sums(scratch, grad, length):
    return jnp.concatenate(
        [
            jnp.sum(grad * scratch[8 - tap : length + 8 - tap, :], axis=0, keepdims=True)
            for tap in range(3)
        ],
        axis=0,
    )


def last_kernel(
    q_in, k_in, v_in, rim_qk, rim_v, taps_q, taps_k, taps_v, places, factors,
    k4, vb, after, gq, kd, gv_in, grad_q, grad_k, grad_v, taps_out, heads_first, narrow, broad, gk,
):
    head = pl.program_id(0)
    length = q_in.shape[1]
    later, total = unpack(after[...])
    later_high, later_low = halves(later)
    value = vb[...]
    value_high = value[:, :VD]
    select = selectors(places[...], head)
    first, second = expand(k4[...], select, factors[...])
    phi_grad = (
        mm(
            jnp.concatenate([value_high, value_high], axis=1),
            jnp.concatenate([later_high, later_low], axis=1),
            1,
            1,
        )
        + mm(value[:, VD:], later_high, 1, 1)
        + total
    )
    key_grad = pull(phi_grad * second, phi_grad * first, select)

    @pl.when(head == 0)
    def _():
        gk[...] = kd[...] + key_grad

    @pl.when(head > 0)
    def _():
        gk[...] += key_grad

    value_grad = gv_in[...] + mm((first * second).astype(BF16), later_high, 1, 0)
    grad_v[...] = conv_back(broad, value_grad, taps_v[...], length)
    extend(broad, v_in[...], rim_v[8:, :].astype(F32))
    sums = tap_sums(broad, value_grad, length)
    heads = heads_first.shape[1] // VD - 1
    for index in range(heads):

        @pl.when(head == index)
        def _(index=index):
            taps_out[3 * index : 3 * index + 3, :] = sums
            heads_first[:, (index + 1) * VD : (index + 2) * VD] = value_grad[0:2, :]

    @pl.when(head == pl.num_programs(0) - 1)
    def _():
        rim = rim_qk[8:, :].astype(F32)
        found = []
        for source, taps, edge, grad, target in (
            (q_in, taps_q, rim[:, :64], gq[...], grad_q),
            (k_in, taps_k, rim[:, 64:], gk[...], grad_k),
        ):
            target[...] = conv_back(narrow, grad, taps[...], length).T
            extend(narrow, source[...].astype(F32).T, edge)
            found.append(tap_sums(narrow, grad, length))
        taps_out[3 * heads : 3 * heads + 3, :] = jnp.concatenate(found, axis=1)
        taps_out[3 * heads + 3 :, :] = jnp.zeros((13 - 3 * heads, VD), F32)
        heads_first[:, :VD] = jnp.concatenate([gq[0:2, :], gk[0:2, :]], axis=1)


def rim_kernel(tail, taps_q, taps_k, taps_v, q_in, k_in, v_in, grad_q, grad_k, grad_v):
    tails = tail[...]
    for start, taps, source, target in (
        (0, taps_q, q_in, grad_q),
        (64, taps_k, k_in, grad_k),
        (128, taps_v, v_in, grad_v),
    ):
        width = taps.shape[1]
        row = lax.broadcasted_iota(jnp.int32, (8, width), 0)
        one, two = tails[0:1, start : start + width], tails[1:2, start : start + width]
        weights = taps[...]
        extra = jnp.where(row == 6, weights[2:3, :] * one, 0.0)
        extra = extra + jnp.where(row == 7, weights[1:2, :] * one + weights[2:3, :] * two, 0.0)
        if start < 128:
            extra = jnp.concatenate([jnp.zeros((120, width), F32), extra], axis=0).T
        target[...] = source[...] + extra


def from_behind(block, axis, distance):
    devices = range(lax.axis_size(axis))
    route = [(i - distance, i) for i in devices if i - distance in devices]
    return lax.ppermute(block, axis, route)


def carried_in(packed, reverse, ahead=()):
    ranks = lax.axis_size(SEQ)
    everyone = lax.all_to_all(packed.reshape(ranks, -1), SEQ, 0, 0, tiled=True)
    rows = lax.broadcasted_iota(jnp.int32, (ranks, ranks), 0)
    cols = lax.broadcasted_iota(jnp.int32, (ranks, ranks), 1)
    reached = (cols > rows) if reverse else (cols < rows)
    sums = jnp.dot(reached.astype(F32), everyone, precision=HIGHEST)
    if ahead:
        sums, ahead = lax.optimization_barrier((sums, ahead))
    return lax.all_to_all(sums, SEQ, 0, 0, tiled=True).reshape(packed.shape), ahead


def turned(block, axis, distance):
    size = lax.axis_size(axis)
    return lax.ppermute(block, axis, [(i, (i + distance) % size) for i in range(size)])


def gathered(block, axis):
    size, index, rows = lax.axis_size(axis), lax.axis_index(axis), block.shape[0]
    whole = jnp.zeros((size * rows,) + block.shape[1:], block.dtype)
    for distance in range(size):
        part = turned(block, axis, distance) if distance else block
        source = (index - distance) % size
        whole = lax.dynamic_update_slice_in_dim(whole, part, source * rows, 0)
    return whole


def scattered(whole, axis):
    size, index = lax.axis_size(axis), lax.axis_index(axis)
    rows = whole.shape[0] // size
    total = lax.dynamic_slice_in_dim(whole, index * rows, rows, 0)
    for distance in range(1, size):
        target = (index + distance) % size
        part = lax.dynamic_slice_in_dim(whole, target * rows, rows, 0)
        total = total + turned(part, axis, distance)
    return total


def to_all(block, axis):
    copies = jnp.broadcast_to(block[None], (lax.axis_size(axis),) + block.shape)
    return lax.all_to_all(copies, axis, 0, 0, tiled=True)


def total_over(block, axis):
    everyone = to_all(block, axis).reshape((lax.axis_size(axis),) + block.shape)
    return jnp.sum(everyone, axis=0)


def body(query_in, key_in, value_in, conv_query, conv_key, conv_value, out_proj, out_grad):
    length, keys = query_in.shape
    heads = conv_value.shape[1] // VD
    assert keys == heads * FK == 64
    places, factors = (jnp.asarray(t) for t in tables())

    def whole(*shape):
        return pl.BlockSpec(shape, lambda h: (0,) * len(shape))

    def per_head(rows):
        return pl.BlockSpec((rows, VD), lambda h: (0, h))

    pairs = pl.BlockSpec((length, 2 * VD), lambda h: (0, h))
    packs = pl.BlockSpec((ROWS, VD), lambda h: (h, 0))
    table = whole(8, WIDE)
    pieces = whole(length, WIDE)
    narrow = whole(length, keys)

    def arr(rows, cols, dtype=F32):
        return jax.ShapeDtypeStruct((rows, cols), dtype)

    def call(kernel, name, ins, outs, shapes, flops, scratch=()):
        return pl.pallas_call(
            kernel,
            name=name,
            grid=(heads,),
            in_specs=ins,
            out_specs=outs,
            out_shape=shapes,
            scratch_shapes=list(scratch),
            cost_estimate=pl.CostEstimate(
                flops=flops, bytes_accessed=4 << 20, transcendentals=0
            ),
        )

    values = heads * VD
    query_cols, key_cols = query_in.T, key_in.T
    upright = whole(keys, length)
    final = [
        pl.BlockSpec((keys, VD), lambda i: (0, length // VD - 1)),
        pl.BlockSpec((keys, VD), lambda i: (0, length // VD - 1)),
        pl.BlockSpec((16, values), lambda i: (length // 16 - 1, 0)),
    ]
    rim = pl.pallas_call(
        rim_rows,
        name="edge",
        grid=(1,),
        in_specs=final,
        out_specs=whole(16, 2 * keys + values),
        out_shape=arr(16, 2 * keys + values, BF16),
    )(query_cols, key_cols, value_in)
    rim = from_behind(rim, SEQ, 1)
    weights = [whole(3, keys), whole(3, keys), per_head(3), table, table]
    weight_args = (conv_query, conv_key, conv_value, places, factors)
    inputs = (query_cols, key_cols, value_in)
    input_specs = [upright, upright, per_head(length)]
    rim_specs = [whole(16, 2 * keys), pl.BlockSpec((16, VD), lambda h: (0, h + 1))]
    conv_ins = input_specs + rim_specs + weights
    conv_args = inputs + (rim, rim) + weight_args
    buffers = [pltpu.VMEM((length + 8, keys), F32), pltpu.VMEM((length + 8, VD), F32)]
    pairs_of = [pieces, pieces, pieces, pairs, packs]
    shapes_of = [arr(length, WIDE, BF16)] * 3 + [
        arr(length, 2 * values, BF16), arr(heads * ROWS, VD),
    ]
    begun = call(
        first_kernel, "first", input_specs + weights, pairs_of, shapes_of, 2 << 30, buffers
    )(*inputs, *weight_args)
    top = whole(16, WIDE)
    corner = whole(keys, VD)
    untouched = pl.BlockSpec(memory_space=pl.ANY)
    q4, k4, k5, vb, local_state = pl.pallas_call(
        mend_kernel,
        name="mend",
        grid=(heads,),
        in_specs=[corner, corner, per_head(16)] + rim_specs + weights + [untouched] * 4 + [packs],
        out_specs=[top, top, top, pl.BlockSpec((16, 2 * VD), lambda h: (0, h)), packs],
        out_shape=shapes_of,
        scratch_shapes=[pltpu.VMEM((24, keys), F32), pltpu.VMEM((24, VD), F32)],
        input_output_aliases={10: 0, 11: 1, 12: 2, 13: 3, 14: 4},
    )(*conv_args, *begun)
    cotangent = gathered(out_grad, "head")
    upstream = lax.dot_general(
        cotangent, out_proj, (((1,), (1,)), ((), ())), preferred_element_type=F32
    )
    numer, denom = call(
        local_kernel, "local", [pieces, pieces, pairs],
        [per_head(length)] * 2, [arr(length, values)] * 2, 4 << 30,
    )(q4, k5, vb)
    before, _ = carried_in(local_state, False)
    att, ng, dg, grad_state = call(
        middle_kernel, "middle",
        [pieces, packs] + [per_head(length)] * 3 + [table, table],
        [per_head(length)] * 3 + [packs],
        [arr(length, values, BF16), arr(length, values), arr(length, values)]
        + [arr(heads * ROWS, VD)],
        4 << 30,
    )(q4, before, numer, denom, upstream, places, factors)
    gq, kd, gv = call(
        inner_kernel, "inner",
        [pieces] * 3 + [pairs, packs] + [per_head(length)] * 2 + [table, table],
        [narrow, narrow, per_head(length)],
        [arr(length, keys)] * 2 + [arr(length, values)],
        8 << 30,
    )(q4, k4, k5, vb, before, ng, dg, places, factors)
    after, (gq, kd, gv) = carried_in(grad_state, True, (gq, kd, gv))
    partial = jnp.dot(att, out_proj, preferred_element_type=F32)
    mixed = scattered(partial, "head").astype(BF16)
    grad_query, grad_key, grad_value, taps, first_rows = call(
        last_kernel, "last",
        conv_ins + [pieces, pairs, packs, narrow, narrow, per_head(length)],
        [upright, upright, per_head(length), whole(16, VD), whole(2, 2 * keys + values)],
        [arr(keys, length)] * 2
        + [arr(length, values), arr(16, VD), arr(2, 2 * keys + values)],
        4 << 30, buffers + [pltpu.VMEM((length, keys), F32)],
    )(*conv_args, k4, vb, after, gq, kd, gv)
    tail = from_behind(first_rows, SEQ, -1)
    taps = total_over(taps, "z")
    rims = [
        pl.BlockSpec((keys, VD), lambda i: (0, length // VD - 1)),
        pl.BlockSpec((keys, VD), lambda i: (0, length // VD - 1)),
        pl.BlockSpec((8, values), lambda i: (length // 8 - 1, 0)),
    ]
    grad_query, grad_key, grad_value = pl.pallas_call(
        rim_kernel,
        name="rims",
        grid=(1,),
        in_specs=[whole(2, 2 * keys + values), whole(3, keys), whole(3, keys), whole(3, values)]
        + rims,
        out_specs=rims,
        out_shape=[arr(keys, length)] * 2 + [arr(length, values)],
        input_output_aliases={4: 0, 5: 1, 6: 2},
    )(tail, conv_query, conv_key, conv_value, grad_query, grad_key, grad_value)
    taps, mixed, grad_query, grad_key, grad_value = lax.optimization_barrier(
        (taps, mixed, grad_query, grad_key, grad_value)
    )
    taps = total_over(taps, ("x", "core"))
    value_taps = taps[: 3 * heads].reshape(heads, 3, VD).transpose(1, 0, 2).reshape(3, values)
    other_taps = taps[3 * heads : 3 * heads + 3]
    return (
        mixed,
        grad_query.T,
        grad_key.T,
        grad_value,
        other_taps[:, :keys],
        other_taps[:, keys:],
        value_taps,
    )


def refined(mesh):
    ranks, groups = mesh.devices.shape
    shape = (4, 16, 2, groups) if ranks == 128 else (1, ranks // 2, 2, groups)
    return Mesh(mesh.devices.reshape(shape), SEQ + ("head",))


def solution(mesh):
    mesh = refined(mesh)
    in_specs = (
        P(SEQ, "head"),
        P(SEQ, "head"),
        P(SEQ, "head"),
        P(None, "head"),
        P(None, "head"),
        P(None, "head"),
        P("head", None),
        P(SEQ + ("head",), None),
    )
    out_specs = (
        P(SEQ + ("head",), None),
        P(SEQ, "head"),
        P(SEQ, "head"),
        P(SEQ, "head"),
        P(None, "head"),
        P(None, "head"),
        P(None, "head"),
    )
    return jax.shard_map(body, mesh=mesh, in_specs=in_specs, out_specs=out_specs, check_vma=False)
```

```python
import jax
import jax.numpy as jnp
import numpy as np
from jax import lax
from jax.experimental import pallas as pl
from jax.experimental.pallas import tpu as pltpu
from jax.sharding import Mesh, PartitionSpec as P

FK = 16
VD = 128
FEAT = 153
ROWS = 160
WIDE = 256
SUMS = FEAT

TOGETHER = {"first": 4, "local": 2, "middle": 2, "inner": 4, "last": 4, "finish": 2}
SEQ = ("x", "z", "core")
HIGHEST = lax.Precision.HIGHEST
F32 = jnp.float32
BF16 = jnp.bfloat16


def tables():
    places = np.full((8, WIDE), -1, np.int32)
    factors = np.zeros((8, WIDE), np.float32)
    factors[0, 0] = 1.0
    factors[0, 1 : FK + 1] = 0.25
    places[0, 1 : FK + 1] = np.arange(FK)
    factors[1, 0] = 1.0
    factors[2, : FK + 1] = 1.0
    column = FK + 1
    for i in range(FK):
        for j in range(i, FK):
            places[0, column], places[1, column] = i, j
            factors[0, column] = 1.0 / 32.0 if i == j else 1.0 / 16.0
            column += 1
    return places, factors


def mm(a, b, ca, cb):
    return lax.dot_general(a, b, (((ca,), (cb,)), ((), ())), preferred_element_type=F32)


def halves(x):
    high = x.astype(BF16)
    return high, (x - high.astype(F32)).astype(BF16)


def fold(pair):
    return pair[:, :VD] + pair[:, VD:]


def when(condition):
    if isinstance(condition, bool):
        return (lambda f: f()) if condition else (lambda f: None)
    return pl.when(condition)


def selectors(places, head):
    row = lax.broadcasted_iota(jnp.int32, (64, WIDE), 0)
    channel = jnp.where((row >> 4) == head, row & 15, -2)
    return tuple(
        jnp.where(channel == places[i : i + 1, :], 1.0, 0.0).astype(BF16) for i in (0, 1)
    )


def tall(select):
    return jnp.concatenate([select, select, select, jnp.zeros_like(select)], axis=0)


def head_lanes(head, width):
    lane = lax.broadcasted_iota(jnp.int32, (1, width), 1)
    return jnp.where(((lane >> 4) & 3) == head, 1.0, 0.0)


def expand(pieces, select, factors):
    return (
        mm(pieces, tall(select[0]), 1, 0) + factors[1:2, :],
        mm(pieces, tall(select[1]), 1, 0) + factors[2:3, :],
    )


def pull(grad_first, grad_second, select):
    return mm(grad_first.astype(BF16), select[0], 1, 1) + mm(
        grad_second.astype(BF16), select[1], 1, 1
    )


def pack(state, total):
    row = lax.broadcasted_iota(jnp.int32, (ROWS, VD), 0)
    state = jnp.where(row == SUMS, total[:, :VD], state[:ROWS, :])
    return jnp.where(row == SUMS + 1, total[:, VD:], state)


def unpack(packed):
    total = jnp.concatenate([packed[SUMS : SUMS + 1, :], packed[SUMS + 1 : SUMS + 2, :]], axis=1)
    return jnp.concatenate([packed, jnp.zeros((WIDE - ROWS, VD), F32)], axis=0), total


def similar(query_pieces, key_pieces, head):
    mine = (query_pieces.astype(F32) * head_lanes(head, WIDE)).astype(BF16)
    return mm(mine, key_pieces, 1, 1) * 0.25


def direct(high, low):
    return high[:, :64] + high[:, 64:128] + low[:, :64]


def causal_mask(length):
    return lax.broadcasted_iota(jnp.int32, (length, length), 0) >= lax.broadcasted_iota(
        jnp.int32, (length, length), 1
    )


def extend(scratch, rows, rim):
    length = rows.shape[0]
    scratch[0:8, :] = rim
    scratch[8 : length + 8, :] = rows.astype(F32)


def convolve(scratch, taps, length):
    total = taps[0:1, :] * scratch[8 : length + 8, :]
    total = total + taps[1:2, :] * scratch[7 : length + 7, :]
    return total + taps[2:3, :] * scratch[6 : length + 6, :]


def rim_rows(q_in, k_in, v_in, out):
    pair = jnp.concatenate([q_in[...].astype(F32), k_in[...].astype(F32)], axis=0).T
    out[:, :VD] = pair[-16:, :].astype(BF16)
    out[:, VD:] = v_in[...]


def split_query(x, target):
    high = x.astype(BF16).astype(F32)
    rest = x - high
    mid = rest.astype(BF16).astype(F32)
    target[:, :128] = jnp.concatenate([high, mid], axis=1).astype(BF16)
    target[:, 128:] = jnp.concatenate([rest - mid, high], axis=1).astype(BF16)
    return high, mid


def split_key(x, target, similar_target):
    high, mid = split_query(x, target)
    similar_target[:, :128] = jnp.concatenate([high, high], axis=1).astype(BF16)
    similar_target[:, 128:] = jnp.concatenate([high, mid], axis=1).astype(BF16)


def first_kernel(
    head, q_in, k_in, v_in, rim_qk, rim_v, taps_q, taps_k, taps_v, places, factors,
    q4, k4, k5, vb, state, narrow, broad,
):
    length = q_in.shape[1]

    @when(head == 0)
    def _():
        rim = rim_qk[8:, :].astype(F32)
        extend(narrow, q_in[...].astype(F32).T, rim[:, :64])
        split_query(convolve(narrow, taps_q[...], length), q4)
        extend(narrow, k_in[...].astype(F32).T, rim[:, 64:])
        split_key(convolve(narrow, taps_k[...], length), k4, k5)

    extend(broad, v_in[...], rim_v[8:, :].astype(F32))
    value = jnp.concatenate(halves(convolve(broad, taps_v[...], length)), axis=1)
    vb[...] = value
    first, second = expand(k4[...], selectors(places[...], head), factors[...])
    phi = (first * second).astype(BF16)
    state[...] = pack(
        fold(mm(phi, value, 0, 0)), jnp.sum(phi.astype(F32), axis=0, keepdims=True)
    )


def local_kernel(head, q4, k5, vb, numer, denom):
    a = similar(q4[...], k5[...], head)
    length = a.shape[0]
    weight = jnp.where(causal_mask(length), 1.0 + a + 0.5 * a * a, 0.0)
    high, low = halves(weight)
    value = vb[...]
    numer[...] = fold(mm(high, value, 1, 0)) + mm(low, value[:, :VD], 1, 0)
    denom[...] = jnp.broadcast_to(jnp.sum(weight, axis=1, keepdims=True), (length, VD))


def middle_kernel(head, q4, before, numer, denom, up, places, factors, att, ng, dg, state):
    scale = factors[...]
    first, second = expand(q4[...], selectors(places[...], head), scale)
    phi = first * second * scale[0:1, :]
    high, low = halves(phi)
    seen, total = unpack(before[...])
    seen_high, seen_low = halves(seen)
    inter = mm(high, seen_high, 1, 0) + mm(high, seen_low, 1, 0) + mm(low, seen_high, 1, 0)
    inverse = 1.0 / (denom[...] + jnp.sum(phi * total, axis=1, keepdims=True))
    out = (numer[...] + inter) * inverse
    att[...] = out.astype(BF16)
    upstream = up[...]
    numer_grad = upstream * inverse
    denom_grad = -jnp.sum(numer_grad * out, axis=1, keepdims=True)
    ng[...] = numer_grad
    dg[...] = jnp.broadcast_to(denom_grad, dg.shape)
    state[...] = pack(
        mm(high, numer_grad.astype(BF16), 0, 0),
        jnp.sum(high.astype(F32) * denom_grad, axis=0, keepdims=True),
    )


def inner_kernel(head, q4, k4, k5, vb, before, ng, dg, places, factors, gq, kd, gv):
    scale = factors[...]
    query, value = q4[...], vb[...]
    a = similar(query, k5[...], head)
    mask = causal_mask(a.shape[0])
    numer_grad = ng[...]
    denom_grad = dg[:, 0:1]
    high, low = halves(numer_grad)
    both = jnp.concatenate([high, low], axis=1)
    value_high, value_low = value[:, :VD], value[:, VD:]
    weight_grad = (
        mm(both, jnp.concatenate([value_high, value_high], axis=1), 1, 1)
        + mm(high, value_low, 1, 1)
        + denom_grad
    )
    sim_high, sim_low = halves(jnp.where(mask, weight_grad * (0.25 + 0.25 * a), 0.0))
    weight = jnp.where(mask, 1.0 + a + 0.5 * a * a, 0.0).astype(BF16)
    gv[...] = mm(weight, high, 0, 0)
    lanes = head_lanes(head, 64)
    key = k4[...]
    query_direct = direct(mm(sim_high, key, 1, 0), mm(sim_low, key, 1, 0)) * lanes
    key_direct = direct(mm(sim_high, query, 0, 0), mm(sim_low, query, 0, 0)) * lanes
    select = selectors(places[...], head)
    first, second = expand(query, select, scale)
    seen, total = unpack(before[...])
    seen_high, seen_low = halves(seen)
    phi_grad = (
        mm(both, jnp.concatenate([seen_high, seen_high], axis=1), 1, 1)
        + mm(high, seen_low, 1, 1)
        + denom_grad * total
    ) * scale[0:1, :]
    query_grad = query_direct + pull(phi_grad * second, phi_grad * first, select)

    @when(head == 0)
    def _():
        gq[...] = query_grad
        kd[...] = key_direct

    @when(head > 0)
    def _():
        gq[...] += query_grad
        kd[...] += key_direct


def conv_back(scratch, grad, tail, taps):
    length, width = grad.shape
    scratch[0:length, :] = grad
    scratch[length : length + 8, :] = jnp.concatenate([tail, jnp.zeros((6, width), F32)], axis=0)
    return (
        taps[0:1, :] * grad
        + taps[1:2, :] * scratch[1 : length + 1, :]
        + taps[2:3, :] * scratch[2 : length + 2, :]
    )


def finish_kernel(
    head, tail_qk, tail_v, taps_q, taps_k, taps_v, gq, gk, gv, grad_q, grad_k, grad_v,
    narrow, broad,
):
    @when(head == 0)
    def _():
        tail = tail_qk[...]
        grad_q[...] = conv_back(narrow, gq[...], tail[:, :64], taps_q[...]).T
        grad_k[...] = conv_back(narrow, gk[...], tail[:, 64:], taps_k[...]).T

    grad_v[...] = conv_back(broad, gv[...], tail_v[...], taps_v[...])


def tap_sums(scratch, grad, length):
    return jnp.concatenate(
        [
            jnp.sum(grad * scratch[8 - tap : length + 8 - tap, :], axis=0, keepdims=True)
            for tap in range(3)
        ],
        axis=0,
    )


def last_kernel(
    head, q_in, k_in, v_in, rim_qk, rim_v, places, factors,
    k4, vb, after, gq, kd, gv_in, gk, gv, taps_out, heads_first, narrow, broad,
):
    length = q_in.shape[1]
    later, total = unpack(after[...])
    later_high, later_low = halves(later)
    value = vb[...]
    value_high = value[:, :VD]
    select = selectors(places[...], head)
    first, second = expand(k4[...], select, factors[...])
    phi_grad = (
        mm(
            jnp.concatenate([value_high, value_high], axis=1),
            jnp.concatenate([later_high, later_low], axis=1),
            1,
            1,
        )
        + mm(value[:, VD:], later_high, 1, 1)
        + total
    )
    key_grad = pull(phi_grad * second, phi_grad * first, select)

    @when(head == 0)
    def _():
        gk[...] = kd[...] + key_grad

    @when(head > 0)
    def _():
        gk[...] += key_grad

    value_grad = gv_in[...] + mm((first * second).astype(BF16), later_high, 1, 0)
    gv[...] = value_grad
    extend(broad, v_in[...], rim_v[8:, :].astype(F32))
    sums = tap_sums(broad, value_grad, length)
    heads = heads_first.shape[1] // VD - 1
    for index in range(heads):

        @when(head == index)
        def _(index=index):
            taps_out[3 * index : 3 * index + 3, :] = sums
            heads_first[:, (index + 1) * VD : (index + 2) * VD] = value_grad[0:2, :]

    @when(head == heads - 1)
    def _():
        rim = rim_qk[8:, :].astype(F32)
        found = []
        for source, edge, grad in (
            (q_in, rim[:, :64], gq[...]),
            (k_in, rim[:, 64:], gk[...]),
        ):
            extend(narrow, source[...].astype(F32).T, edge)
            found.append(tap_sums(narrow, grad, length))
        taps_out[3 * heads : 3 * heads + 3, :] = jnp.concatenate(found, axis=1)
        taps_out[3 * heads + 3 :, :] = jnp.zeros((13 - 3 * heads, VD), F32)
        heads_first[:, :VD] = jnp.concatenate([gq[0:2, :], gk[0:2, :]], axis=1)


def from_behind(block, axis, distance):
    devices = range(lax.axis_size(axis))
    route = [(i - distance, i) for i in devices if i - distance in devices]
    return lax.ppermute(block, axis, route)


def carried_in(packed, reverse, ahead=()):
    ranks = lax.axis_size(SEQ)
    everyone = lax.all_to_all(packed.reshape(ranks, -1), SEQ, 0, 0, tiled=True)
    rows = lax.broadcasted_iota(jnp.int32, (ranks, ranks), 0)
    cols = lax.broadcasted_iota(jnp.int32, (ranks, ranks), 1)
    reached = (cols > rows) if reverse else (cols < rows)
    sums = jnp.dot(reached.astype(F32), everyone, precision=HIGHEST)
    if ahead:
        sums, ahead = lax.optimization_barrier((sums, ahead))
    return lax.all_to_all(sums, SEQ, 0, 0, tiled=True).reshape(packed.shape), ahead


def turned(block, axis, distance):
    size = lax.axis_size(axis)
    return lax.ppermute(block, axis, [(i, (i + distance) % size) for i in range(size)])


def gathered(block, axis):
    size, index, rows = lax.axis_size(axis), lax.axis_index(axis), block.shape[0]
    whole = jnp.zeros((size * rows,) + block.shape[1:], block.dtype)
    for distance in range(size):
        part = turned(block, axis, distance) if distance else block
        source = (index - distance) % size
        whole = lax.dynamic_update_slice_in_dim(whole, part, source * rows, 0)
    return whole


def scattered(whole, axis):
    size, index = lax.axis_size(axis), lax.axis_index(axis)
    rows = whole.shape[0] // size
    total = lax.dynamic_slice_in_dim(whole, index * rows, rows, 0)
    for distance in range(1, size):
        target = (index + distance) % size
        part = lax.dynamic_slice_in_dim(whole, target * rows, rows, 0).astype(BF16)
        total = total + turned(part, axis, distance).astype(F32)
    return total


def to_all(block, axis):
    copies = jnp.broadcast_to(block[None], (lax.axis_size(axis),) + block.shape)
    return lax.all_to_all(copies, axis, 0, 0, tiled=True)


def total_over(block, axis):
    everyone = to_all(block, axis).reshape((lax.axis_size(axis),) + block.shape)
    return jnp.sum(everyone, axis=0)


def body(query_in, key_in, value_in, conv_query, conv_key, conv_value, out_proj, out_grad):
    length, keys = query_in.shape
    heads = conv_value.shape[1] // VD
    assert keys == heads * FK == 64
    places, factors = (jnp.asarray(t) for t in tables())

    def whole(*shape):
        return pl.BlockSpec(shape, lambda h: (0,) * len(shape))

    def per_head(rows, width=VD):
        return ("lanes", rows, width)

    pairs = per_head(length, 2 * VD)
    packs = ("rows", ROWS, VD)
    table = whole(8, WIDE)
    pieces = whole(length, WIDE)
    narrow = whole(length, keys)

    def arr(rows, cols, dtype=F32):
        return jax.ShapeDtypeStruct((rows, cols), dtype)

    def call(kernel, name, together, ins, outs, shapes, flops, scratch=(), aliases=None):
        kinds = [spec[0] if isinstance(spec, tuple) else "whole" for spec in ins + outs]

        def spec_of(spec):
            if not isinstance(spec, tuple):
                return spec
            kind, rows, width = spec
            if kind == "lanes":
                return pl.BlockSpec((rows, together * width), lambda h: (0, h))
            if kind == "rows":
                return pl.BlockSpec((together * rows, width), lambda h: (h, 0))
            return whole(rows, width)

        def step(*refs):
            for sub in range(together):
                head = sub if together == heads else pl.program_id(0) * together + sub
                views = []
                for kind, spec, ref in zip(kinds, ins + outs, refs):
                    if kind == "lanes":
                        ref = ref.at[:, sub * spec[2] : (sub + 1) * spec[2]]
                    elif kind == "rows":
                        ref = ref.at[sub * spec[1] : (sub + 1) * spec[1], :]
                    elif kind == "rim":
                        start = (head + 1) * VD
                        if together < heads:
                            start = pl.multiple_of(start, VD)
                        ref = ref.at[:, pl.ds(start, VD)]
                    views.append(ref)
                kernel(head, *views, *refs[len(kinds) :])

        return pl.pallas_call(
            step,
            name=name,
            grid=(heads // together,),
            in_specs=[spec_of(spec) for spec in ins],
            out_specs=[spec_of(spec) for spec in outs],
            out_shape=shapes,
            scratch_shapes=list(scratch),
            input_output_aliases=aliases or {},
            cost_estimate=pl.CostEstimate(
                flops=flops, bytes_accessed=4 << 20, transcendentals=0
            ),
        )

    values = heads * VD
    query_cols, key_cols = query_in.T, key_in.T
    upright = whole(keys, length)
    final = [
        pl.BlockSpec((keys, VD), lambda i: (0, length // VD - 1)),
        pl.BlockSpec((keys, VD), lambda i: (0, length // VD - 1)),
        pl.BlockSpec((16, values), lambda i: (length // 16 - 1, 0)),
    ]
    rim = pl.pallas_call(
        rim_rows,
        name="edge",
        grid=(1,),
        in_specs=final,
        out_specs=whole(16, 2 * keys + values),
        out_shape=arr(16, 2 * keys + values, BF16),
    )(query_cols, key_cols, value_in)
    rim = from_behind(rim, SEQ, 1)
    weights = [whole(3, keys), whole(3, keys), per_head(3), table, table]
    weight_args = (conv_query, conv_key, conv_value, places, factors)
    inputs = (query_cols, key_cols, value_in)
    input_specs = [upright, upright, per_head(length)]
    rim_specs = [whole(16, 2 * keys), ("rim", 16, 2 * keys + values)]
    conv_ins = input_specs + rim_specs + weights
    conv_args = inputs + (rim, rim) + weight_args
    buffers = [pltpu.VMEM((length + 8, keys), F32), pltpu.VMEM((length + 8, VD), F32)]
    pairs_of = [pieces, pieces, pieces, pairs, packs]
    shapes_of = [arr(length, WIDE, BF16)] * 3 + [
        arr(length, 2 * values, BF16), arr(heads * ROWS, VD),
    ]
    q4, k4, k5, vb, local_state = call(
        first_kernel, "first", TOGETHER["first"], conv_ins, pairs_of, shapes_of, 2 << 30, buffers
    )(*conv_args)
    cotangent = gathered(out_grad, "head")
    upstream = lax.dot_general(
        cotangent, out_proj, (((1,), (1,)), ((), ())), preferred_element_type=F32
    )
    numer, denom = call(
        local_kernel, "local", TOGETHER["local"], [pieces, pieces, pairs],
        [per_head(length)] * 2, [arr(length, values)] * 2, 4 << 30,
    )(q4, k5, vb)
    before, _ = carried_in(local_state, False)
    att, ng, dg, grad_state = call(
        middle_kernel, "middle", TOGETHER["middle"],
        [pieces, packs] + [per_head(length)] * 3 + [table, table],
        [per_head(length)] * 3 + [packs],
        [arr(length, values, BF16), arr(length, values), arr(length, values)]
        + [arr(heads * ROWS, VD)],
        4 << 30,
    )(q4, before, numer, denom, upstream, places, factors)
    gq, kd, gv = call(
        inner_kernel, "inner", TOGETHER["inner"],
        [pieces] * 3 + [pairs, packs] + [per_head(length)] * 2 + [table, table],
        [narrow, narrow, per_head(length)],
        [arr(length, keys)] * 2 + [arr(length, values)],
        8 << 30,
    )(q4, k4, k5, vb, before, ng, dg, places, factors)
    after, (gq, kd, gv) = carried_in(grad_state, True, (gq, kd, gv))
    partial = jnp.dot(att, out_proj, preferred_element_type=F32)
    mixed = scattered(partial, "head").astype(BF16)
    gk, gv, taps, first_rows = call(
        last_kernel, "last", TOGETHER["last"],
        input_specs + rim_specs + [table, table]
        + [pieces, pairs, packs, narrow, narrow, per_head(length)],
        [narrow, per_head(length), whole(16, VD), whole(2, 2 * keys + values)],
        [arr(length, keys), arr(length, values), arr(16, VD), arr(2, 2 * keys + values)],
        4 << 30, buffers,
    )(*inputs, rim, rim, places, factors, k4, vb, after, gq, kd, gv)
    first_rows, mixed = lax.optimization_barrier((first_rows, mixed))
    tail = from_behind(first_rows, SEQ, -1)
    taps = total_over(taps, "z")
    taps, tail = lax.optimization_barrier((taps, tail))
    grad_query, grad_key, grad_value = call(
        finish_kernel, "finish", TOGETHER["finish"],
        [whole(2, 2 * keys), ("rim", 2, 2 * keys + values)] + weights[:3]
        + [narrow, narrow, per_head(length)],
        [upright, upright, per_head(length)],
        [arr(keys, length)] * 2 + [arr(length, values)],
        1 << 24, buffers,
    )(tail, tail, conv_query, conv_key, conv_value, gq, gk, gv)
    taps = total_over(taps, ("x", "core"))
    value_taps = taps[: 3 * heads].reshape(heads, 3, VD).transpose(1, 0, 2).reshape(3, values)
    other_taps = taps[3 * heads : 3 * heads + 3]
    return (
        mixed,
        grad_query.T,
        grad_key.T,
        grad_value,
        other_taps[:, :keys],
        other_taps[:, keys:],
        value_taps,
    )


def refined(mesh):
    ranks, groups = mesh.devices.shape
    shape = (4, 16, 2, groups) if ranks == 128 else (1, ranks // 2, 2, groups)
    return Mesh(mesh.devices.reshape(shape), SEQ + ("head",))


def solution(mesh):
    mesh = refined(mesh)
    in_specs = (
        P(SEQ, "head"),
        P(SEQ, "head"),
        P(SEQ, "head"),
        P(None, "head"),
        P(None, "head"),
        P(None, "head"),
        P("head", None),
        P(SEQ + ("head",), None),
    )
    out_specs = (
        P(SEQ + ("head",), None),
        P(SEQ, "head"),
        P(SEQ, "head"),
        P(SEQ, "head"),
        P(None, "head"),
        P(None, "head"),
        P(None, "head"),
    )
    return jax.shard_map(body, mesh=mesh, in_specs=in_specs, out_specs=out_specs, check_vma=False)
```

```python
import jax
import jax.numpy as jnp
import numpy as np
from jax import lax
from jax.experimental import pallas as pl
from jax.experimental.pallas import tpu as pltpu
from jax.sharding import Mesh, PartitionSpec as P

FK = 16
VD = 128
FEAT = 153
ROWS = 160
WIDE = 256
SUMS = FEAT

TOGETHER = {"first": 4, "local": 2, "middle": 2, "inner": 4, "last": 4, "finish": 2}
SEQ = ("x", "z", "core")
HIGHEST = lax.Precision.HIGHEST
F32 = jnp.float32
BF16 = jnp.bfloat16


def tables():
    places = np.full((8, WIDE), -1, np.int32)
    factors = np.zeros((8, WIDE), np.float32)
    factors[0, 0] = 1.0
    factors[0, 1 : FK + 1] = 0.25
    places[0, 1 : FK + 1] = np.arange(FK)
    factors[1, 0] = 1.0
    factors[2, : FK + 1] = 1.0
    column = FK + 1
    for i in range(FK):
        for j in range(i, FK):
            places[0, column], places[1, column] = i, j
            factors[0, column] = 1.0 / 32.0 if i == j else 1.0 / 16.0
            column += 1
    return places, factors


def mm(a, b, ca, cb):
    return lax.dot_general(a, b, (((ca,), (cb,)), ((), ())), preferred_element_type=F32)


def halves(x):
    high = x.astype(BF16)
    return high, (x - high.astype(F32)).astype(BF16)


def fold(pair):
    return pair[:, :VD] + pair[:, VD:]


def when(condition):
    if isinstance(condition, bool):
        return (lambda f: f()) if condition else (lambda f: None)
    return pl.when(condition)


def selectors(places, head):
    row = lax.broadcasted_iota(jnp.int32, (64, WIDE), 0)
    channel = jnp.where((row >> 4) == head, row & 15, -2)
    return tuple(
        jnp.where(channel == places[i : i + 1, :], 1.0, 0.0).astype(BF16) for i in (0, 1)
    )


def tall(select):
    return jnp.concatenate([select, select, select, jnp.zeros_like(select)], axis=0)


def head_lanes(head, width):
    lane = lax.broadcasted_iota(jnp.int32, (1, width), 1)
    return jnp.where(((lane >> 4) & 3) == head, 1.0, 0.0)


def expand(pieces, select, factors):
    return (
        mm(pieces, tall(select[0]), 1, 0) + factors[1:2, :],
        mm(pieces, tall(select[1]), 1, 0) + factors[2:3, :],
    )


def pull(grad_first, grad_second, select):
    return mm(grad_first.astype(BF16), select[0], 1, 1) + mm(
        grad_second.astype(BF16), select[1], 1, 1
    )


def pack(state, total):
    row = lax.broadcasted_iota(jnp.int32, (ROWS, VD), 0)
    state = jnp.where(row == SUMS, total[:, :VD], state[:ROWS, :])
    return jnp.where(row == SUMS + 1, total[:, VD:], state)


def unpack(packed):
    total = jnp.concatenate([packed[SUMS : SUMS + 1, :], packed[SUMS + 1 : SUMS + 2, :]], axis=1)
    return jnp.concatenate([packed, jnp.zeros((WIDE - ROWS, VD), F32)], axis=0), total


def similar(query_pieces, key_pieces, head):
    mine = (query_pieces.astype(F32) * head_lanes(head, WIDE)).astype(BF16)
    return mm(mine, key_pieces, 1, 1) * 0.25


def direct(high, low):
    return high[:, :64] + high[:, 64:128] + low[:, :64]


def causal_mask(length):
    return lax.broadcasted_iota(jnp.int32, (length, length), 0) >= lax.broadcasted_iota(
        jnp.int32, (length, length), 1
    )


def extend(scratch, rows, rim):
    length = rows.shape[0]
    scratch[0:8, :] = rim
    scratch[8 : length + 8, :] = rows.astype(F32)


def convolve(scratch, taps, length):
    total = taps[0:1, :] * scratch[8 : length + 8, :]
    total = total + taps[1:2, :] * scratch[7 : length + 7, :]
    return total + taps[2:3, :] * scratch[6 : length + 6, :]


def rim_rows(q_in, k_in, v_in, out):
    pair = jnp.concatenate([q_in[...].astype(F32), k_in[...].astype(F32)], axis=0).T
    out[:, :VD] = pair[-16:, :].astype(BF16)
    out[:, VD:] = v_in[...]


def split_query(x, target):
    high = x.astype(BF16).astype(F32)
    rest = x - high
    mid = rest.astype(BF16).astype(F32)
    target[:, :128] = jnp.concatenate([high, mid], axis=1).astype(BF16)
    target[:, 128:] = jnp.concatenate([rest - mid, high], axis=1).astype(BF16)
    return high, mid


def split_key(x, target, similar_target):
    high, mid = split_query(x, target)
    similar_target[:, :128] = jnp.concatenate([high, high], axis=1).astype(BF16)
    similar_target[:, 128:] = jnp.concatenate([high, mid], axis=1).astype(BF16)


def first_kernel(
    head, q_in, k_in, v_in, rim_qk, rim_v, taps_q, taps_k, taps_v, places, factors,
    q4, k4, k5, vb, state, narrow, broad,
):
    length = q_in.shape[1]

    @when(head == 0)
    def _():
        rim = rim_qk[8:, :].astype(F32)
        extend(narrow, q_in[...].astype(F32).T, rim[:, :64])
        split_query(convolve(narrow, taps_q[...], length), q4)
        extend(narrow, k_in[...].astype(F32).T, rim[:, 64:])
        split_key(convolve(narrow, taps_k[...], length), k4, k5)

    extend(broad, v_in[...], rim_v[8:, :].astype(F32))
    value = jnp.concatenate(halves(convolve(broad, taps_v[...], length)), axis=1)
    vb[...] = value
    first, second = expand(k4[...], selectors(places[...], head), factors[...])
    phi = (first * second).astype(BF16)
    state[...] = pack(
        fold(mm(phi, value, 0, 0)), jnp.sum(phi.astype(F32), axis=0, keepdims=True)
    )


def local_kernel(head, q4, k5, vb, numer, denom):
    a = similar(q4[...], k5[...], head)
    length = a.shape[0]
    weight = jnp.where(causal_mask(length), 1.0 + a + 0.5 * a * a, 0.0)
    high, low = halves(weight)
    value = vb[...]
    numer[...] = fold(mm(high, value, 1, 0)) + mm(low, value[:, :VD], 1, 0)
    denom[...] = jnp.broadcast_to(jnp.sum(weight, axis=1, keepdims=True), (length, VD))


def middle_kernel(head, q4, before, numer, denom, up, places, factors, att, ng, dg, state):
    scale = factors[...]
    first, second = expand(q4[...], selectors(places[...], head), scale)
    phi = first * second * scale[0:1, :]
    high, low = halves(phi)
    seen, total = unpack(before[...])
    seen_high, seen_low = halves(seen)
    inter = mm(high, seen_high, 1, 0) + mm(high, seen_low, 1, 0) + mm(low, seen_high, 1, 0)
    inverse = 1.0 / (denom[...] + jnp.sum(phi * total, axis=1, keepdims=True))
    out = (numer[...] + inter) * inverse
    att[...] = out.astype(BF16)
    upstream = up[...]
    numer_grad = upstream * inverse
    denom_grad = -jnp.sum(numer_grad * out, axis=1, keepdims=True)
    ng[...] = numer_grad
    dg[...] = jnp.broadcast_to(denom_grad, dg.shape)
    state[...] = pack(
        mm(high, numer_grad.astype(BF16), 0, 0),
        jnp.sum(high.astype(F32) * denom_grad, axis=0, keepdims=True),
    )


def inner_kernel(head, q4, k4, k5, vb, before, ng, dg, places, factors, gq, kd, gv):
    scale = factors[...]
    query, value = q4[...], vb[...]
    a = similar(query, k5[...], head)
    mask = causal_mask(a.shape[0])
    numer_grad = ng[...]
    denom_grad = dg[:, 0:1]
    high, low = halves(numer_grad)
    both = jnp.concatenate([high, low], axis=1)
    value_high, value_low = value[:, :VD], value[:, VD:]
    weight_grad = (
        mm(both, jnp.concatenate([value_high, value_high], axis=1), 1, 1)
        + mm(high, value_low, 1, 1)
        + denom_grad
    )
    sim_high, sim_low = halves(jnp.where(mask, weight_grad * (0.25 + 0.25 * a), 0.0))
    weight = jnp.where(mask, 1.0 + a + 0.5 * a * a, 0.0).astype(BF16)
    gv[...] = mm(weight, high, 0, 0)
    lanes = head_lanes(head, 64)
    key = k4[...]
    query_direct = direct(mm(sim_high, key, 1, 0), mm(sim_low, key, 1, 0)) * lanes
    key_direct = direct(mm(sim_high, query, 0, 0), mm(sim_low, query, 0, 0)) * lanes
    select = selectors(places[...], head)
    first, second = expand(query, select, scale)
    seen, total = unpack(before[...])
    seen_high, seen_low = halves(seen)
    phi_grad = (
        mm(both, jnp.concatenate([seen_high, seen_high], axis=1), 1, 1)
        + mm(high, seen_low, 1, 1)
        + denom_grad * total
    ) * scale[0:1, :]
    query_grad = query_direct + pull(phi_grad * second, phi_grad * first, select)

    @when(head == 0)
    def _():
        gq[...] = query_grad
        kd[...] = key_direct

    @when(head > 0)
    def _():
        gq[...] += query_grad
        kd[...] += key_direct


def conv_back(scratch, grad, tail, taps):
    length, width = grad.shape
    scratch[0:length, :] = grad
    scratch[length : length + 8, :] = jnp.concatenate([tail, jnp.zeros((6, width), F32)], axis=0)
    return (
        taps[0:1, :] * grad
        + taps[1:2, :] * scratch[1 : length + 1, :]
        + taps[2:3, :] * scratch[2 : length + 2, :]
    )


def finish_kernel(
    head, tail_qk, tail_v, taps_q, taps_k, taps_v, gq, gk, gv, grad_q, grad_k, grad_v,
    narrow, broad,
):
    @when(head == 0)
    def _():
        tail = tail_qk[...]
        grad_q[...] = conv_back(narrow, gq[...], tail[:, :64], taps_q[...]).T
        grad_k[...] = conv_back(narrow, gk[...], tail[:, 64:], taps_k[...]).T

    grad_v[...] = conv_back(broad, gv[...], tail_v[...], taps_v[...])


def tap_sums(scratch, grad, length):
    return jnp.concatenate(
        [
            jnp.sum(grad * scratch[8 - tap : length + 8 - tap, :], axis=0, keepdims=True)
            for tap in range(3)
        ],
        axis=0,
    )


def last_kernel(
    head, q_in, k_in, v_in, rim_qk, rim_v, places, factors,
    k4, vb, after, gq, kd, gv_in, gk, gv, taps_out, heads_first, narrow, broad,
):
    length = q_in.shape[1]
    later, total = unpack(after[...])
    later_high, later_low = halves(later)
    value = vb[...]
    value_high = value[:, :VD]
    select = selectors(places[...], head)
    first, second = expand(k4[...], select, factors[...])
    phi_grad = (
        mm(
            jnp.concatenate([value_high, value_high], axis=1),
            jnp.concatenate([later_high, later_low], axis=1),
            1,
            1,
        )
        + mm(value[:, VD:], later_high, 1, 1)
        + total
    )
    key_grad = pull(phi_grad * second, phi_grad * first, select)

    @when(head == 0)
    def _():
        gk[...] = kd[...] + key_grad

    @when(head > 0)
    def _():
        gk[...] += key_grad

    value_grad = gv_in[...] + mm((first * second).astype(BF16), later_high, 1, 0)
    gv[...] = value_grad
    extend(broad, v_in[...], rim_v[8:, :].astype(F32))
    sums = tap_sums(broad, value_grad, length)
    heads = heads_first.shape[1] // VD - 1
    for index in range(heads):

        @when(head == index)
        def _(index=index):
            taps_out[3 * index : 3 * index + 3, :] = sums
            heads_first[:, (index + 1) * VD : (index + 2) * VD] = value_grad[0:2, :]

    @when(head == heads - 1)
    def _():
        rim = rim_qk[8:, :].astype(F32)
        found = []
        for source, edge, grad in (
            (q_in, rim[:, :64], gq[...]),
            (k_in, rim[:, 64:], gk[...]),
        ):
            extend(narrow, source[...].astype(F32).T, edge)
            found.append(tap_sums(narrow, grad, length))
        taps_out[3 * heads : 3 * heads + 3, :] = jnp.concatenate(found, axis=1)
        taps_out[3 * heads + 3 : 16, :] = jnp.zeros((13 - 3 * heads, VD), F32)
        block = taps_out[0:16, :]
        for copy in range(1, taps_out.shape[0] // 16):
            taps_out[16 * copy : 16 * copy + 16, :] = block
        heads_first[:, :VD] = jnp.concatenate([gq[0:2, :], gk[0:2, :]], axis=1)


def from_behind(block, axis, distance):
    devices = range(lax.axis_size(axis))
    route = [(i - distance, i) for i in devices if i - distance in devices]
    return lax.ppermute(block, axis, route)


def carried_in(packed, reverse, ahead=()):
    ranks = lax.axis_size(SEQ)
    everyone = lax.all_to_all(packed.reshape(ranks, -1), SEQ, 0, 0, tiled=True)
    rows = lax.broadcasted_iota(jnp.int32, (ranks, ranks), 0)
    cols = lax.broadcasted_iota(jnp.int32, (ranks, ranks), 1)
    reached = (cols > rows) if reverse else (cols < rows)
    sums = jnp.dot(reached.astype(F32), everyone, precision=HIGHEST)
    if ahead:
        sums, ahead = lax.optimization_barrier((sums, ahead))
    return lax.all_to_all(sums, SEQ, 0, 0, tiled=True).reshape(packed.shape), ahead


def turned(block, axis, distance):
    size = lax.axis_size(axis)
    return lax.ppermute(block, axis, [(i, (i + distance) % size) for i in range(size)])


def gathered(block, axis):
    size, index, rows = lax.axis_size(axis), lax.axis_index(axis), block.shape[0]
    whole = jnp.zeros((size * rows,) + block.shape[1:], block.dtype)
    for distance in range(size):
        part = turned(block, axis, distance) if distance else block
        source = (index - distance) % size
        whole = lax.dynamic_update_slice_in_dim(whole, part, source * rows, 0)
    return whole


def scattered(whole, axis):
    size, index = lax.axis_size(axis), lax.axis_index(axis)
    rows = whole.shape[0] // size
    total = lax.dynamic_slice_in_dim(whole, index * rows, rows, 0)
    for distance in range(1, size):
        target = (index + distance) % size
        part = lax.dynamic_slice_in_dim(whole, target * rows, rows, 0).astype(BF16)
        total = total + turned(part, axis, distance).astype(F32)
    return total


def to_all(block, axis):
    copies = jnp.broadcast_to(block[None], (lax.axis_size(axis),) + block.shape)
    return lax.all_to_all(copies, axis, 0, 0, tiled=True)


def total_over(block, axis):
    everyone = to_all(block, axis).reshape((lax.axis_size(axis),) + block.shape)
    return jnp.sum(everyone, axis=0)


def body(query_in, key_in, value_in, conv_query, conv_key, conv_value, out_proj, out_grad):
    length, keys = query_in.shape
    heads = conv_value.shape[1] // VD
    assert keys == heads * FK == 64
    places, factors = (jnp.asarray(t) for t in tables())

    def whole(*shape):
        return pl.BlockSpec(shape, lambda h: (0,) * len(shape))

    def per_head(rows, width=VD):
        return ("lanes", rows, width)

    pairs = per_head(length, 2 * VD)
    packs = ("rows", ROWS, VD)
    table = whole(8, WIDE)
    pieces = whole(length, WIDE)
    narrow = whole(length, keys)

    def arr(rows, cols, dtype=F32):
        return jax.ShapeDtypeStruct((rows, cols), dtype)

    def call(kernel, name, together, ins, outs, shapes, flops, scratch=(), aliases=None):
        kinds = [spec[0] if isinstance(spec, tuple) else "whole" for spec in ins + outs]

        def spec_of(spec):
            if not isinstance(spec, tuple):
                return spec
            kind, rows, width = spec
            if kind == "lanes":
                return pl.BlockSpec((rows, together * width), lambda h: (0, h))
            if kind == "rows":
                return pl.BlockSpec((together * rows, width), lambda h: (h, 0))
            return whole(rows, width)

        def step(*refs):
            for sub in range(together):
                head = sub if together == heads else pl.program_id(0) * together + sub
                views = []
                for kind, spec, ref in zip(kinds, ins + outs, refs):
                    if kind == "lanes":
                        ref = ref.at[:, sub * spec[2] : (sub + 1) * spec[2]]
                    elif kind == "rows":
                        ref = ref.at[sub * spec[1] : (sub + 1) * spec[1], :]
                    elif kind == "rim":
                        start = (head + 1) * VD
                        if together < heads:
                            start = pl.multiple_of(start, VD)
                        ref = ref.at[:, pl.ds(start, VD)]
                    views.append(ref)
                kernel(head, *views, *refs[len(kinds) :])

        return pl.pallas_call(
            step,
            name=name,
            grid=(heads // together,),
            in_specs=[spec_of(spec) for spec in ins],
            out_specs=[spec_of(spec) for spec in outs],
            out_shape=shapes,
            scratch_shapes=list(scratch),
            input_output_aliases=aliases or {},
            cost_estimate=pl.CostEstimate(
                flops=flops, bytes_accessed=4 << 20, transcendentals=0
            ),
        )

    values = heads * VD
    query_cols, key_cols = query_in.T, key_in.T
    upright = whole(keys, length)
    final = [
        pl.BlockSpec((keys, VD), lambda i: (0, length // VD - 1)),
        pl.BlockSpec((keys, VD), lambda i: (0, length // VD - 1)),
        pl.BlockSpec((16, values), lambda i: (length // 16 - 1, 0)),
    ]
    rim = pl.pallas_call(
        rim_rows,
        name="edge",
        grid=(1,),
        in_specs=final,
        out_specs=whole(16, 2 * keys + values),
        out_shape=arr(16, 2 * keys + values, BF16),
    )(query_cols, key_cols, value_in)
    rim = from_behind(rim, SEQ, 1)
    weights = [whole(3, keys), whole(3, keys), per_head(3), table, table]
    weight_args = (conv_query, conv_key, conv_value, places, factors)
    inputs = (query_cols, key_cols, value_in)
    input_specs = [upright, upright, per_head(length)]
    rim_specs = [whole(16, 2 * keys), ("rim", 16, 2 * keys + values)]
    conv_ins = input_specs + rim_specs + weights
    conv_args = inputs + (rim, rim) + weight_args
    buffers = [pltpu.VMEM((length + 8, keys), F32), pltpu.VMEM((length + 8, VD), F32)]
    pairs_of = [pieces, pieces, pieces, pairs, packs]
    shapes_of = [arr(length, WIDE, BF16)] * 3 + [
        arr(length, 2 * values, BF16), arr(heads * ROWS, VD),
    ]
    q4, k4, k5, vb, local_state = call(
        first_kernel, "first", TOGETHER["first"], conv_ins, pairs_of, shapes_of, 2 << 30, buffers
    )(*conv_args)
    cotangent = gathered(out_grad, "head")
    upstream = lax.dot_general(
        cotangent, out_proj, (((1,), (1,)), ((), ())), preferred_element_type=F32
    )
    numer, denom = call(
        local_kernel, "local", TOGETHER["local"], [pieces, pieces, pairs],
        [per_head(length)] * 2, [arr(length, values)] * 2, 4 << 30,
    )(q4, k5, vb)
    before, _ = carried_in(local_state, False)
    att, ng, dg, grad_state = call(
        middle_kernel, "middle", TOGETHER["middle"],
        [pieces, packs] + [per_head(length)] * 3 + [table, table],
        [per_head(length)] * 3 + [packs],
        [arr(length, values, BF16), arr(length, values), arr(length, values)]
        + [arr(heads * ROWS, VD)],
        4 << 30,
    )(q4, before, numer, denom, upstream, places, factors)
    gq, kd, gv = call(
        inner_kernel, "inner", TOGETHER["inner"],
        [pieces] * 3 + [pairs, packs] + [per_head(length)] * 2 + [table, table],
        [narrow, narrow, per_head(length)],
        [arr(length, keys)] * 2 + [arr(length, values)],
        8 << 30,
    )(q4, k4, k5, vb, before, ng, dg, places, factors)
    after, (gq, kd, gv) = carried_in(grad_state, True, (gq, kd, gv))
    partial = jnp.dot(att, out_proj, preferred_element_type=F32)
    mixed = scattered(partial, "head").astype(BF16)
    along = lax.axis_size("z")
    gk, gv, taps, first_rows = call(
        last_kernel, "last", TOGETHER["last"],
        input_specs + rim_specs + [table, table]
        + [pieces, pairs, packs, narrow, narrow, per_head(length)],
        [narrow, per_head(length), whole(16 * along, VD), whole(2, 2 * keys + values)],
        [arr(length, keys), arr(length, values), arr(16 * along, VD), arr(2, 2 * keys + values)],
        4 << 30, buffers,
    )(*inputs, rim, rim, places, factors, k4, vb, after, gq, kd, gv)
    first_rows, mixed = lax.optimization_barrier((first_rows, mixed))
    tail = from_behind(first_rows, SEQ, -1)
    taps = lax.all_to_all(taps.reshape(along, 16, VD), "z", 0, 0, tiled=True)
    taps = jnp.sum(taps, axis=0)
    taps, tail = lax.optimization_barrier((taps, tail))
    grad_query, grad_key, grad_value = call(
        finish_kernel, "finish", TOGETHER["finish"],
        [whole(2, 2 * keys), ("rim", 2, 2 * keys + values)] + weights[:3]
        + [narrow, narrow, per_head(length)],
        [upright, upright, per_head(length)],
        [arr(keys, length)] * 2 + [arr(length, values)],
        1 << 24, buffers,
    )(tail, tail, conv_query, conv_key, conv_value, gq, gk, gv)
    taps = total_over(taps, ("x", "core"))
    value_taps = taps[: 3 * heads].reshape(heads, 3, VD).transpose(1, 0, 2).reshape(3, values)
    other_taps = taps[3 * heads : 3 * heads + 3]
    return (
        mixed,
        grad_query.T,
        grad_key.T,
        grad_value,
        other_taps[:, :keys],
        other_taps[:, keys:],
        value_taps,
    )


def refined(mesh):
    ranks, groups = mesh.devices.shape
    shape = (4, 16, 2, groups) if ranks == 128 else (1, ranks // 2, 2, groups)
    return Mesh(mesh.devices.reshape(shape), SEQ + ("head",))


def solution(mesh):
    mesh = refined(mesh)
    in_specs = (
        P(SEQ, "head"),
        P(SEQ, "head"),
        P(SEQ, "head"),
        P(None, "head"),
        P(None, "head"),
        P(None, "head"),
        P("head", None),
        P(SEQ + ("head",), None),
    )
    out_specs = (
        P(SEQ + ("head",), None),
        P(SEQ, "head"),
        P(SEQ, "head"),
        P(SEQ, "head"),
        P(None, "head"),
        P(None, "head"),
        P(None, "head"),
    )
    return jax.shard_map(body, mesh=mesh, in_specs=in_specs, out_specs=out_specs, check_vma=False)
```
